256 devices in a mesh: dp: 4 (over y), expert: 64 (over x, z, core).
Axes of the slice: x: 4, y: 4, z: 8, core: 2. Of those that a mesh axis runs over, the one named last changes fastest.
Arguments:
- tokens: bfloat16 [6144, 4096], P(('dp', 'expert')), may hold values from -6 to 6
- out_grad: bfloat16 [6144, 4096], P(('dp', 'expert')), may hold values from -6 to 6
- routes: int32 [6144, 8], P(('dp', 'expert')), may hold values from 0 to 63, all different within a row; in each aligned block of 24 rows (0 to 23, 24 to 47, ...) at most 4 rows name the same one
- gates: bfloat16 [6144, 8], P(('dp', 'expert')), may hold values from 0.099609375 to 0.5
- w_gate: bfloat16 [64, 768, 4096], P('expert', 'dp'), may hold values from -0.09375 to 0.09375
- w_up: bfloat16 [64, 768, 4096], P('expert', 'dp'), may hold values from -0.09375 to 0.09375
- w_down: bfloat16 [64, 768, 4096], P('expert', 'dp'), may hold values from -0.21875 to 0.21875
Outputs:
- d_tokens: bfloat16 [6144, 4096], P(('dp', 'expert'))
- d_gate: bfloat16 [64, 768, 4096], P('expert', 'dp')
- d_up: bfloat16 [64, 768, 4096], P('expert', 'dp')
- d_down: bfloat16 [64, 768, 4096], P('expert', 'dp')
The draws below stay inside these ranges and needn't reach their ends.
Inputs may be any that keep to these rules, and one draw needn't show every extreme that they name: `routes`: each row names 8 different experts. Within the 24 rows of one device no expert is named by more than 4 rows, and in every draw some expert is named by exactly 4 rows of some device.
All inputs are finite; a program needn't handle non-finite values.
Results may differ from the reference program's by a relative error of at most 0.015.
Values may be sent and summed in bfloat16 or wider, within the bound.
A program may use at most 128 MiB of HBM per device.

```python
import math
import jax
import jax.numpy as jnp
import numpy as np
from jax import lax

D = 4096
HIDDEN_SIZE = 768
TOP_K = 8
TOK_DEV = 24
EXPERTS = 64
CAP = 4
TOKENS = 6144
N_DP = 4


def level_of(own_key, extent, split, least, largest):
    def one(axis_at, blocks):
        steps = jax.random.uniform(jax.random.fold_in(jax.random.fold_in(own_key, 6), axis_at), (blocks,), jnp.float32, least / len(split), largest / len(split))
        return jnp.repeat(jnp.exp(steps), extent[axis_at] // blocks).reshape((-1,) + (1,) * (len(extent) - axis_at - 1))

    gain = one(*split[0])
    for cut in split[1:]:
        gain = gain * one(*cut)
    return gain


def shared_out(rng, own, number, rows, number_of, top, most, slope):
    order = jax.random.permutation(rng, number_of)
    crowded, ordinary = shares(number_of, rows * top, most, slope, True), shares(number_of, rows * top, most, slope, False)
    places = jnp.arange(number_of)

    def named(lengths, rotation):
        used = int((lengths > 0).sum())
        fixed = max(1, used // 4)
        moved = fixed + (places - fixed + rotation * (used - fixed)) % max(1, number_of - fixed)
        return jnp.zeros((number_of,), jnp.int32).at[order[jnp.where(places < fixed, places, moved)]].set(jnp.asarray(lengths, jnp.int32))

    lengths = jnp.where(number % 4 == 0, named(crowded, number // 4), named(ordinary, number - number // 4 - 1))
    mixed = jax.random.permutation(jax.random.fold_in(own, 3), number_of)
    donor, taker = mixed[0:number_of // 2 * 2:2], mixed[1:number_of // 2 * 2:2]
    slack = jnp.minimum(lengths[donor] - 1, most - lengths[taker]) // 2
    slack = jnp.where((donor == order[0]) | (taker == order[0]) | (lengths[taker] == 0), 0, jnp.maximum(slack, 0))
    moved = jax.random.randint(jax.random.fold_in(own, 4), (number_of // 2,), 0, 1 << 20) % (slack + 1)
    lengths = lengths.at[donor].add(-moved).at[taker].add(moved)
    items = jnp.searchsorted(jnp.cumsum(lengths), jnp.arange(rows * top), side="right").astype(jnp.int32)
    table = items.reshape(top, rows).T
    table = table[jax.random.permutation(jax.random.fold_in(own, 1), rows)]
    rotation = jax.random.randint(jax.random.fold_in(own, 2), (rows, 1), 0, top)
    return jnp.take_along_axis(table, (jnp.arange(top)[None, :] + rotation) % top, axis=1)


def shares(number_of, total, bound, lean, full):
    portions = [(1 << 20) // math.isqrt(standing ** lean) + 1 for standing in range(1, number_of + 1)]
    largest = bound if full else min(bound, max(-(-total // number_of), total * portions[0] // sum(portions)))
    least = 1 if total - largest >= number_of - 1 else 0
    holding, rest = [largest] + [least] * (number_of - 1), total - largest - least * (number_of - 1)
    while rest > 0:
        movable = [i for i in range(1, number_of) if holding[i] < largest] or [i for i in range(1, number_of) if holding[i] < bound]
        pool, left = sum([portions[i] for i in movable]), rest
        for i in movable:
            addition = min(bound - holding[i], max(1, left * portions[i] // pool), rest)
            holding[i] = holding[i] + addition
            rest = rest - addition
    return np.array(holding)


def bell_draw(own_key, shape, scale, limit, pieces=(), kind=jnp.bfloat16):
    drawn = jax.random.normal(own_key, shape, jnp.float32) * scale
    if len(pieces) > 0:
        drawn = level_of(own_key, shape, pieces, -0.22, 0.18) * drawn
    return jnp.clip(drawn, min=-limit, max=limit).astype(kind)


def setup_inputs(seed: int = 0) -> dict:
    key_list = jax.random.split(jax.random.key(seed), 8)
    tokens = bell_draw(key_list[0], (TOKENS, D), 1.0, 6.0, ((0, 256),))
    out_grad = bell_draw(key_list[1], (TOKENS, D), 1.0, 6.0, ((0, 256),))
    routes_keys = jax.random.split(jax.random.fold_in(key_list[2], 1), TOKENS // TOK_DEV)
    routes_turns = jax.random.permutation(jax.random.fold_in(key_list[2], 3), TOKENS // TOK_DEV)
    routes = jax.vmap(lambda own, number: shared_out(jax.random.fold_in(key_list[2], 2), own, number, TOK_DEV, EXPERTS, TOP_K, CAP, 2))(routes_keys, routes_turns).reshape((TOKENS, TOP_K))
    gates = jnp.clip(0.099609375 + 0.40039062 * jax.random.uniform(key_list[3], (TOKENS, TOP_K), jnp.float32) ** level_of(key_list[3], (TOKENS, TOP_K), ((0, 256),), -0.2, 0.2), 0.099609375, 0.5).astype(jnp.bfloat16)
    w_gate = bell_draw(key_list[4], (EXPERTS, HIDDEN_SIZE, D), D ** -0.5, 0.09375, ((0, 64), (1, 4)))
    w_up = bell_draw(key_list[5], (EXPERTS, HIDDEN_SIZE, D), D ** -0.5, 0.09375, ((0, 64), (1, 4)))
    w_down = bell_draw(key_list[6], (EXPERTS, HIDDEN_SIZE, D), HIDDEN_SIZE ** -0.5, 0.21875, ((0, 64), (1, 4)))
    return {"tokens": tokens, "out_grad": out_grad, "routes": routes, "gates": gates, "w_gate": w_gate, "w_up": w_up, "w_down": w_down}


def reference(tokens, out_grad, routes, gates, w_gate, w_up, w_down):
    blocks = TOKENS // TOK_DEV
    quarter = HIDDEN_SIZE // N_DP
    expert_ids = jnp.arange(EXPERTS, dtype=jnp.int32)
    onehot = (routes[:, :, None] == expert_ids).astype(jnp.int32)
    chosen = jnp.sum(onehot, axis=1).astype(jnp.int32).reshape(blocks, TOK_DEV, EXPERTS)
    earlier = (jnp.cumsum(chosen, axis=1).astype(jnp.int32) - chosen).reshape(TOKENS, EXPERTS)
    slot_index = jnp.sum(onehot * earlier[:, None, :], axis=2).astype(jnp.int32)
    source = (jnp.arange(TOKENS, dtype=jnp.int32) // TOK_DEV).astype(jnp.int32)
    place_col = (source[:, None] * CAP + slot_index).astype(jnp.int32)
    pair_ids = jnp.arange(TOKENS * TOP_K, dtype=jnp.int32).reshape(TOKENS, TOP_K)
    table = jnp.full((EXPERTS, blocks * CAP), TOKENS * TOP_K, jnp.int32)
    table = table.at[routes, place_col].set(pair_ids)
    input_ext = jnp.concatenate([tokens, jnp.zeros((1, D), tokens.dtype)], axis=0)
    grad_ext = jnp.concatenate([out_grad, jnp.zeros((1, D), out_grad.dtype)], axis=0)
    gate_ext = jnp.concatenate([gates.reshape(-1).astype(jnp.float32), jnp.zeros((1,), jnp.float32)])

    def expert_step(dx_acc, inputs):
        pair_row, gate_w, up_w, down_w = inputs
        token_row = (pair_row // TOP_K).astype(jnp.int32)
        x_slot = input_ext[token_row]
        g_slot = (gate_ext[pair_row][:, None] * grad_ext[token_row].astype(jnp.float32)).astype(jnp.bfloat16)
        gate_pre = jnp.dot(x_slot, gate_w.T, preferred_element_type=jnp.float32)
        up_pre = jnp.dot(x_slot, up_w.T, preferred_element_type=jnp.float32)
        sigmoid_gate = jax.nn.sigmoid(gate_pre)
        silu_gate = gate_pre * sigmoid_gate
        hidden = (silu_gate * up_pre).astype(jnp.bfloat16)
        d_hidden = jnp.dot(g_slot, down_w.T, preferred_element_type=jnp.float32)
        d_up_act = (d_hidden * silu_gate).astype(jnp.bfloat16)
        d_gate_act = (d_hidden * up_pre * sigmoid_gate * (1.0 + gate_pre * (1.0 - sigmoid_gate))).astype(jnp.bfloat16)
        grad_down = jnp.dot(hidden.T, g_slot, preferred_element_type=jnp.float32).astype(jnp.bfloat16)
        grad_gate = jnp.dot(d_gate_act.T, x_slot, preferred_element_type=jnp.float32).astype(jnp.bfloat16)
        grad_up = jnp.dot(d_up_act.T, x_slot, preferred_element_type=jnp.float32).astype(jnp.bfloat16)
        rows_count = x_slot.shape[0]
        gate_parts = jnp.einsum("rqf,qfd->qrd", d_gate_act.astype(jnp.float32).reshape(rows_count, N_DP, quarter), gate_w.astype(jnp.float32).reshape(N_DP, quarter, D))
        up_parts = jnp.einsum("rqf,qfd->qrd", d_up_act.astype(jnp.float32).reshape(rows_count, N_DP, quarter), up_w.astype(jnp.float32).reshape(N_DP, quarter, D))
        rounded = lax.optimization_barrier((gate_parts + up_parts).astype(jnp.bfloat16))
        dx_slot = jnp.sum(rounded.astype(jnp.float32), axis=0)
        dx_acc = dx_acc.at[token_row].add(dx_slot)
        return dx_acc, (grad_gate, grad_up, grad_down)

    start = jnp.zeros((TOKENS + 1, D), jnp.float32)
    dx_acc, grads = lax.scan(expert_step, start, (table, w_gate, w_up, w_down))
    return dx_acc[:TOKENS].astype(jnp.bfloat16), grads[0], grads[1], grads[2]
```

```python
import jax
import jax.numpy as jnp
from jax import lax
from jax.experimental import pallas as pl
from jax.experimental.pallas import tpu as pltpu
from jax.sharding import PartitionSpec as P

MESH = pl.DeviceIdType.MESH
F32, BF16 = jnp.float32, jnp.bfloat16
VMEM_LIMIT = 67043328

NY, NX, NZ, NCORE = 4, 4, 8, 2
CAP = 4
TOK = 24
PAD = 32
SRC = NX * NCORE
ROWS = NZ * CAP


class Place:
    def __init__(self):
        self.y = lax.axis_index("dp")
        e = lax.axis_index("expert")
        self.c = lax.rem(e, NCORE)
        self.z = lax.rem(lax.div(e, NCORE), NZ)
        self.x = lax.div(e, NCORE * NZ)

    @staticmethod
    def first(i):
        return i + 1 - 2 * lax.rem(i, 2)

    @staticmethod
    def second(i):
        return 3 - i

    def pick(self, i, s):
        return (1 - s) * self.first(i) + s * self.second(i)

    def at(self, y=None, x=None, z=None, c=None):
        y = self.y if y is None else y
        x = self.x if x is None else x
        z = self.z if z is None else z
        c = self.c if c is None else c
        return (y, (x * NZ + z) * NCORE + c)

    def zz(self, d):
        return lax.rem(self.z + d + NZ, NZ)

    def enter(self):
        sem = pltpu.get_barrier_semaphore()
        peers = [self.at(y=self.first(self.y)), self.at(y=self.second(self.y))]
        peers += [self.at(z=self.zz(1)), self.at(z=self.zz(-1)), self.at(c=1 - self.c)]
        for x in (self.first(self.x), self.second(self.x)):
            peers += [self.at(x=x, c=0), self.at(x=x, c=1)]
        for p in peers:
            pl.semaphore_signal(sem, inc=1, device_id=p, device_id_type=MESH)
        pl.semaphore_wait(sem, len(peers))


def send(src, dst, ssem, rsem, device):
    pltpu.make_async_remote_copy(
        src_ref=src, dst_ref=dst, send_sem=ssem, recv_sem=rsem, device_id=device, device_id_type=MESH
    ).start()


def await_(ref, sem):
    pltpu.make_async_copy(ref, ref, sem).wait()


def when(i, n):
    return pl.when(jnp.logical_and(i >= 0, i < n))


def dot(a, b, dims=((1,), (0,))):
    return lax.dot_general(a, b, (dims, ((), ())), preferred_element_type=F32)


def slot_exchange(p, s, i, sel, fwd, into, send_sem, fwd_send, fwd_recv, recv_sem):
    mine = p.c
    send(sel.at[i, :, 1 - mine], into.at[:, mine], send_sem, recv_sem, p.at(c=1 - mine))
    send(sel.at[i, :, pl.ds(6, 2)], fwd.at[i], send_sem, fwd_recv, p.at(x=p.pick(p.x, s)))
    for d, x in ((1, p.first(p.x)), (2, p.second(p.x))):
        for c in range(NCORE):
            send(sel.at[i, :, d * 2 + c], into.at[:, d * 2 + mine], send_sem, recv_sem, p.at(x=x, c=c))


def pass_on(p, s, i, fwd, into, fwd_send, recv_sem):
    for c in range(NCORE):
        send(fwd.at[i, :, c], into.at[:, 6 + p.c], fwd_send, recv_sem, p.at(x=p.pick(p.x, 1 - s), c=c))


def quarter(pos, s):
    return (0, 1 + s, 2 - s, 3)[pos]


def route_stage(tok, info, wg, wu, wd, rows_out, act_t_out, act_out, st_out,
                zbuf, sel, fwd, rows, wgu, wdn, acc_gu, acc_d, sm, rb,
                sem_l, a_s, a_r, z_s, z_r, x_s, x_r, f_s, f_r, l_s, l_r, o_s, r_s, r_r):
    p = Place()
    n, _, w = tok.shape
    half = n // 2
    hid = wg.shape[0]
    y1, y2 = p.first(p.y), p.second(p.y)

    own_tok = pltpu.make_async_copy(tok, zbuf.at[:, 0, p.z], sem_l.at[0])
    own_tok.start()
    own_info = pltpu.make_async_copy(info, rb.at[0, p.z], sem_l.at[1])
    own_info.start()
    loads = [
        pltpu.make_async_copy(wg, wgu.at[pl.ds(0, hid)], sem_l.at[2]),
        pltpu.make_async_copy(wu, wgu.at[pl.ds(hid, hid)], sem_l.at[3]),
        pltpu.make_async_copy(wd, wdn, sem_l.at[4]),
    ]
    for cp in loads:
        cp.start()
    p.enter()
    send(info, rb.at[1, p.z], r_s.at[7], r_r.at[7], p.at(y=y1))
    send(info, rb.at[2, p.z], r_s.at[8], r_r.at[8], p.at(y=y2))

    @pl.loop(0, n)
    def _(i):
        send(tok.at[i], zbuf.at[i, 1, p.z], a_s.at[i], a_r.at[i], p.at(y=p.pick(p.y, lax.rem(i, 2))))

    acc_gu[...] = jnp.zeros_like(acc_gu)
    acc_d[...] = jnp.zeros_like(acc_d)

    def z_hop(buf, k, ssem, rsem):
        for side, d in ((0, 1), (1, -1)):
            block = p.zz(-d * (k - 1))
            send(buf.at[:, block], buf.at[:, block], ssem(2 * (k - 1) + side), rsem.at[2 * (k - 1) + side], p.at(z=p.zz(d)))

    def z_last(buf, s, ssem, rsem):
        d = 1 - 2 * s
        block = p.zz(-3 * d)
        send(buf.at[:, block], buf.at[:, block], ssem(6), rsem.at[6], p.at(z=p.zz(d)))

    def z_wait(buf, k, rsem):
        for side in (0, 1):
            await_(buf.at[:, 0], rsem.at[2 * (k - 1) + side])

    def info_step(t):
        one = lambda j: r_s.at[j]

        @pl.when(t == 0)
        def _():
            own_info.wait()
            await_(info, r_r.at[7])
            await_(info, r_r.at[8])
            z_hop(rb, 1, one, r_r)

        for k in (1, 2):

            @pl.when(t == k)
            def _(k=k):
                z_wait(rb, k, r_r)
                z_hop(rb, k + 1, one, r_r)

        @pl.when(t == 3)
        def _():
            z_wait(rb, 3, r_r)
            z_last(rb, 0, one, r_r)

        @pl.when(t == 4)
        def _():
            await_(rb.at[:, 0], r_r.at[6])
            select_matrices()

    def select_matrices():
        lane = lax.broadcasted_iota(jnp.int32, (128, 128), 1)
        sub = lax.broadcasted_iota(jnp.int32, (128, 128), 0)
        before = jnp.where(jnp.logical_and(sub < lane, lax.div(sub, PAD) == lax.div(lane, PAD)), 1.0, 0.0).astype(BF16)
        r_row = lax.broadcasted_iota(jnp.int32, (ROWS, 128), 0)
        r_lane = lax.broadcasted_iota(jnp.int32, (ROWS, 128), 1)
        row_z, row_slot = lax.div(r_row, CAP), lax.rem(r_row, CAP).astype(F32)
        xs = (p.x, p.first(p.x), p.second(p.x), lax.rem(p.x + 2, NX))
        for role in range(3):
            for zh in range(2):
                both = rb[role, 4 * zh].astype(F32)
                for q in range(1, 4):
                    both = both + rb[role, 4 * zh + q].astype(F32)
                route, gate = both[0:8].astype(jnp.int32), both[8:16]
                chosen, value = [], []
                for d in range(4):
                    for c in range(NCORE):
                        hit = route == (xs[d] * NZ + p.z) * NCORE + c + 1
                        chosen.append(jnp.sum(jnp.where(hit, 1.0, 0.0), axis=0, keepdims=True))
                        value.append(jnp.sum(jnp.where(hit, gate, 0.0), axis=0, keepdims=True))
                chosen = jnp.concatenate(chosen, axis=0)
                earlier = dot(chosen.astype(BF16), before)
                same_z = row_z == 4 * zh + lax.div(r_lane, PAD)
                for e in range(SRC):
                    spread = lambda v: jnp.broadcast_to(v, (ROWS, 128))
                    hit = jnp.logical_and(same_z, jnp.logical_and(spread(chosen[e : e + 1]) > 0.5, spread(earlier[e : e + 1]) == row_slot))
                    place = (pl.ds(e * ROWS, ROWS), pl.ds(zh * 128, 128))
                    sm[0, role, place[0], place[1]] = jnp.where(hit, 1.0, 0.0).astype(BF16)
                    sm[1, role, place[0], place[1]] = jnp.where(hit, spread(value[e]), 0.0).astype(BF16)
            st_out[role] = sm[0, role].astype(F32).T.astype(BF16)

    def step(t, carry):
        i6, i5, i4, i3, i2, i1 = (t - k for k in (6, 5, 4, 3, 2, 1))

        @when(i6, n)
        def _():
            await_(rows.at[i6, 0, :, pl.ds(0, 7)], x_r.at[i6])
            late = p.at(y=p.pick(p.y, 1 - lax.rem(i6, 2)))
            send(rows.at[i6, 0], rows.at[i6, 1], l_s.at[i6], l_r.at[i6], late)

        @when(i5, n)
        def _():
            await_(fwd.at[i5], f_r.at[i5])
            pass_on(p, lax.rem(i5, 2), i5, fwd, rows.at[i5, 0], f_s.at[i5], x_r.at[i5])

        info_step(t)

        @when(i4, n)
        def _():
            s = lax.rem(i4, 2)
            which = lax.div(i4, half)
            await_(zbuf.at[i4, :, 0], z_r.at[i4, 6])
            for ys, role in ((0, 0), (1, 1 + s)):
                got = dot(sm[which, role], zbuf[i4, ys].reshape(NZ * PAD, w)).astype(BF16)
                sel[i4, ys] = got.reshape(SRC, ROWS, w)
            rows[i4, 0, :, p.c] = sel[i4, :, p.c]
            slot_exchange(p, s, i4, sel, fwd, rows.at[i4, 0], x_s.at[i4], f_s.at[i4], f_r.at[i4], x_r.at[i4])

        @when(i3, n)
        def _():
            z_wait(zbuf.at[i3], 3, z_r.at[i3])
            z_last(zbuf.at[i3], lax.rem(i3, 2), lambda j: z_s.at[i3], z_r.at[i3])

        for i, k in ((i2, 2), (i1, 1)):

            @when(i, n)
            def _(i=i, k=k):
                z_wait(zbuf.at[i], k, z_r.at[i])
                z_hop(zbuf.at[i], k + 1, lambda j: z_s.at[i], z_r.at[i])

        @when(t, n)
        def _():
            @pl.when(t == 0)
            def _():
                own_tok.wait()

            await_(tok.at[t], a_r.at[t])
            z_hop(zbuf.at[t], 1, lambda j: z_s.at[t], z_r.at[t])

        i8 = t - 8

        @pl.when(i8 == 0)
        def _():
            for cp in loads:
                cp.wait()

        @when(i8, n)
        def _():
            s = lax.rem(i8, 2)
            await_(rows.at[i8, 1], l_r.at[i8])
            for h in range(2):
                for ys in range(2):
                    k = pl.multiple_of((2 * h + ys) * SRC * ROWS, SRC * ROWS)
                    pltpu.make_async_copy(rows.at[i8, h, ys], rows_out.at[i8, 2 * h + ys], o_s.at[i8, 2 * h + ys]).start()

            def multiply(acc, weights):
                j = lax.rem(i8, half)
                cols = weights[:, pl.ds(pl.multiple_of(j * w, w), w)]
                for h in range(2):
                    for ys in range(2):
                        q = quarter(2 * h + ys, s)
                        at = pl.ds(pl.multiple_of(q * SRC * ROWS, SRC * ROWS), SRC * ROWS)
                        acc[:, at] += dot(cols, rows[i8, h, ys].reshape(SRC * ROWS, w), ((1,), (1,)))

            @pl.when(i8 < half)
            def _():
                multiply(acc_gu, wgu)

            @pl.when(i8 >= half)
            def _():
                multiply(acc_d, wdn)

        return carry

    lax.fori_loop(0, n + 8, step, 0)

    for q in range(4):
        at = pl.ds(q * SRC * ROWS, SRC * ROWS)
        gate_pre, up_pre, d_hidden = acc_gu[0:hid, at], acc_gu[hid : 2 * hid, at], acc_d[:, at]
        sig = jax.nn.sigmoid(gate_pre)
        silu = gate_pre * sig
        d_up = d_hidden * silu
        d_gate = d_hidden * up_pre * sig * (1.0 + gate_pre * (1.0 - sig))
        both = jnp.concatenate([d_gate, d_up], axis=0)
        act_t_out[0 : 2 * hid, at] = both.astype(BF16)
        act_t_out[2 * hid : 3 * hid, at] = (silu * up_pre).astype(BF16)
        act_out[at, :] = both.T.astype(BF16)

    @pl.loop(0, n)
    def _(i):
        await_(tok.at[i], a_s.at[i])
        await_(zbuf.at[i, :, pl.ds(0, 7)], z_s.at[i])
        await_(sel.at[i, :, pl.ds(0, 7)], x_s.at[i])
        await_(fwd.at[i], f_s.at[i])
        await_(rows.at[i, 0], l_s.at[i])
        for k in range(4):
            await_(rows.at[i, 0, 0], o_s.at[i, k])

    for j in range(7):
        await_(rb.at[:, 0], r_s.at[j])
    await_(info, r_s.at[7])
    await_(info, r_s.at[8])


def return_stage(act, act_t, st, wg, wu, rows_in, d_tok, d_gate, d_up, d_down,
                 wgu, acts, keep, part, got, total, fwd, back, own, zs, zr, tail, tail_in, xr, gr, dw_gu, dw_d,
                 sem_l, in_s, l_s, l_r, x_s, x_r, f_s, f_r, z_s, z_r, e_s, e_r, o_s):
    p = Place()
    n, w = keep.shape[0], keep.shape[-1]
    hid = wg.shape[0]
    qr = SRC * ROWS

    loads = [
        pltpu.make_async_copy(wg, wgu.at[pl.ds(0, hid)], sem_l.at[0]),
        pltpu.make_async_copy(wu, wgu.at[pl.ds(hid, hid)], sem_l.at[1]),
    ]
    for cp in loads:
        cp.start()

    def fetch(i, slot):
        pltpu.make_async_copy(rows_in.at[i], xr.at[slot], in_s.at[slot, 0]).start()
        pltpu.make_async_copy(rows_in.at[n + i], gr.at[slot], in_s.at[slot, 1]).start()

    fetch(0, 0)
    p.enter()
    acts[0] = act_t[...]
    for pos in range(4):
        acts[1, :, pl.ds(pos * qr, qr)] = act_t[:, pl.ds(quarter(pos, 1) * qr, qr)]
    for cp in loads:
        cp.wait()

    def z_send(i, k, side, src):
        j = 6 if k == 4 else 2 * (k - 1) + side
        d = 2 * side - 1
        send(src, zr.at[i, j], z_s.at[i, j], z_r.at[i, j], p.at(z=p.zz(d)))

    def step(t, carry):
        i1, i2, i3, i4, i5, i6, i7, i8 = (t - k for k in range(1, 9))

        @when(t, n)
        def _():
            s = lax.rem(t, 2)
            cols = wgu[:, pl.ds(pl.multiple_of(t * w, w), w)]
            for pos in (2, 3, 0, 1):
                q = quarter(pos, s)
                a = act[pl.ds(pl.multiple_of(q * qr, qr), qr), :]
                value = dot(a, cols).astype(BF16).reshape(SRC, ROWS, w)
                if pos >= 2:
                    part[t, pos - 2] = value
                else:
                    keep[t, pos] = value
                if pos == 3:
                    late = p.at(y=p.pick(p.y, 1 - s))
                    send(part.at[t], got.at[t], l_s.at[t], l_r.at[t], late)

        @when(i1, n)
        def _():
            s = lax.rem(i1, 2)
            await_(got.at[i1], l_r.at[i1])
            total[i1] = (keep[i1].astype(F32) + got[i1].astype(F32)).astype(BF16)
            back[i1, :, p.c] = total[i1, :, p.c]
            slot_exchange(p, s, i1, total, fwd, back.at[i1], x_s.at[i1], f_s.at[i1], f_r.at[i1], x_r.at[i1])

        @when(i2, n)
        def _():
            await_(fwd.at[i2], f_r.at[i2])
            pass_on(p, lax.rem(i2, 2), i2, fwd, back.at[i2], f_s.at[i2], x_r.at[i2])

        @when(i3, n)
        def _():
            s = lax.rem(i3, 2)
            await_(back.at[i3, :, pl.ds(0, 7)], x_r.at[i3])
            for ys, role in ((0, 0), (1, 1 + s)):
                value = dot(st[role], back[i3, ys].reshape(qr, w)).astype(BF16)
                own[i3, ys] = value.reshape(NZ, PAD, w)
            block = own.at[i3, :, p.zz(4)]
            d = 2 * s - 1
            send(block, zr.at[i3, 6], z_s.at[i3, 6], z_r.at[i3, 6], p.at(z=p.zz(d)))

        @when(i4, n)
        def _():
            s = lax.rem(i4, 2)
            await_(zr.at[i4, 6], z_r.at[i4, 6])
            four = zr[i4, 6].astype(F32)
            for side in (0, 1):
                mine = own[i4, :, p.zz(3 * (2 * side - 1))].astype(F32)
                add = four * jnp.where(s == side, 1.0, 0.0)
                zs[i4, 4 + side] = (mine + add).astype(BF16)
                z_send(i4, 3, side, zs.at[i4, 4 + side])

        for i, k in ((i5, 2), (i6, 1)):

            @when(i, n)
            def _(i=i, k=k):
                for side in (0, 1):
                    await_(zr.at[i, 0], z_r.at[i, 2 * k + side])
                    mine = own[i, :, p.zz(k * (2 * side - 1))].astype(F32)
                    j = 2 * (k - 1) + side
                    zs[i, j] = (mine + zr[i, 2 * k + side].astype(F32)).astype(BF16)
                    z_send(i, k, side, zs.at[i, j])

        @when(i7, n)
        def _():
            for side in (0, 1):
                await_(zr.at[i7, 0], z_r.at[i7, side])
            value = own[i7, :, p.z].astype(F32) + zr[i7, 0].astype(F32) + zr[i7, 1].astype(F32)
            zs[i7, 6, 0] = value[0].astype(BF16)
            tail[i7] = value[1].astype(BF16)
            send(tail.at[i7], tail_in.at[i7], e_s.at[i7], e_r.at[i7], p.at(y=p.pick(p.y, lax.rem(i7, 2))))

        @when(i8, n)
        def _():
            await_(tail_in.at[i8], e_r.at[i8])
            value = zs[i8, 6, 0].astype(F32) + tail_in[i8].astype(F32)
            d_tok[:, pl.ds(pl.multiple_of(i8 * w, w), w)] = value[0:TOK].astype(BF16)

        @when(t, n)
        def _():
            slot = lax.rem(t, 2)

            @pl.when(t + 1 < n)
            def _():
                fetch(t + 1, 1 - slot)

            await_(xr.at[slot], in_s.at[slot, 0])
            await_(gr.at[slot], in_s.at[slot, 1])
            a = acts[slot]
            x_all = xr[slot].reshape(4 * qr, w)
            g_all = gr[slot].reshape(4 * qr, w)
            dw_gu[t] = dot(a[0 : 2 * hid], x_all).astype(BF16)
            dw_d[t] = dot(a[2 * hid : 3 * hid], g_all).astype(BF16)
            at = pl.ds(pl.multiple_of(t * w, w), w)
            pltpu.make_async_copy(dw_gu.at[t, pl.ds(0, hid)], d_gate.at[:, at], o_s.at[t, 0]).start()
            pltpu.make_async_copy(dw_gu.at[t, pl.ds(hid, hid)], d_up.at[:, at], o_s.at[t, 1]).start()
            pltpu.make_async_copy(dw_d.at[t], d_down.at[:, at], o_s.at[t, 2]).start()

        return carry

    lax.fori_loop(0, n + 8, step, 0)

    @pl.loop(0, n)
    def _(i):
        await_(part.at[i], l_s.at[i])
        await_(total.at[i, :, pl.ds(0, 7)], x_s.at[i])
        await_(fwd.at[i], f_s.at[i])
        for j in range(7):
            await_(zr.at[i, j], z_s.at[i, j])
        await_(tail.at[i], e_s.at[i])
        for j in range(3):
            await_(dw_d.at[i], o_s.at[i, j])


def per_device(tokens, out_grad, routes, gates, w_gate, w_up, w_down):
    width = tokens.shape[1]
    w = 512
    nc = width // w
    n = 2 * nc
    hid = w_gate.shape[1]
    qr = SRC * ROWS
    z = lax.rem(lax.div(lax.axis_index("expert"), NCORE), NZ)

    def chunks(a):
        a = jnp.pad(a, ((0, PAD - TOK), (0, 0)))
        return a.reshape(PAD, nc, w).transpose(1, 0, 2)

    tok = jnp.concatenate([chunks(tokens), chunks(out_grad)], axis=0)
    info = jnp.concatenate([(routes + 1).astype(BF16).T, gates.T], axis=0)
    info = jnp.pad(info, ((0, 0), (0, PAD - TOK)))
    info = jnp.where(lax.broadcasted_iota(jnp.int32, (16, 4, PAD), 1) == lax.rem(z, 4), info[:, None, :], 0).reshape(16, 128)

    anywhere = pl.BlockSpec(memory_space=pl.ANY)
    vmem = pl.BlockSpec(memory_space=pltpu.VMEM)
    dma = pltpu.SemaphoreType.DMA
    shape = jax.ShapeDtypeStruct
    rows, act_t, act, st = pl.pallas_call(
        route_stage,
        out_shape=(shape((n, 4, SRC, ROWS, w), BF16), shape((3 * hid, 4 * qr), BF16), shape((4 * qr, 2 * hid), BF16), shape((3, qr, qr), BF16)),
        in_specs=[anywhere, vmem, anywhere, anywhere, anywhere],
        out_specs=(anywhere, vmem, vmem, vmem),
        scratch_shapes=[
            pltpu.VMEM((n, 2, NZ, PAD, w), BF16),
            pltpu.VMEM((n, 2, SRC, ROWS, w), BF16),
            pltpu.VMEM((n, 2, 2, ROWS, w), BF16),
            pltpu.VMEM((n, 2, 2, SRC, ROWS, w), BF16),
            pltpu.VMEM((2 * hid, width), BF16),
            pltpu.VMEM((hid, width), BF16),
            pltpu.VMEM((2 * hid, 4 * qr), F32),
            pltpu.VMEM((hid, 4 * qr), F32),
            pltpu.VMEM((2, 3, qr, qr), BF16),
            pltpu.VMEM((3, NZ, 16, 128), BF16),
            dma((5,)), dma((n,)), dma((n,)), dma((n,)), dma((n, 7)), dma((n,)), dma((n,)), dma((n,)), dma((n,)),
            dma((n,)), dma((n,)), dma((n, 4)), dma((9,)), dma((9,)),
        ],
        compiler_params=pltpu.CompilerParams(collective_id=0, has_side_effects=True, vmem_limit_bytes=VMEM_LIMIT),
    )(tok, info, w_gate[0], w_up[0], w_down[0])

    n = nc
    d_tok, d_gate, d_up, d_down = pl.pallas_call(
        return_stage,
        out_shape=(shape((TOK, width), BF16),) + (shape((hid, width), BF16),) * 3,
        in_specs=[vmem, vmem, vmem, anywhere, anywhere, anywhere],
        out_specs=(vmem, anywhere, anywhere, anywhere),
        scratch_shapes=[
            pltpu.VMEM((2 * hid, width), BF16),
            pltpu.VMEM((2, 3 * hid, 4 * qr), BF16),
            pltpu.VMEM((n, 2, SRC, ROWS, w), BF16),
            pltpu.VMEM((n, 2, SRC, ROWS, w), BF16),
            pltpu.VMEM((n, 2, SRC, ROWS, w), BF16),
            pltpu.VMEM((n, 2, SRC, ROWS, w), BF16),
            pltpu.VMEM((n, 2, 2, ROWS, w), BF16),
            pltpu.VMEM((n, 2, SRC, ROWS, w), BF16),
            pltpu.VMEM((n, 2, NZ, PAD, w), BF16),
            pltpu.VMEM((n, 7, 2, PAD, w), BF16),
            pltpu.VMEM((n, 7, 2, PAD, w), BF16),
            pltpu.VMEM((n, PAD, w), BF16),
            pltpu.VMEM((n, PAD, w), BF16),
            pltpu.VMEM((2, 4, SRC, ROWS, w), BF16),
            pltpu.VMEM((2, 4, SRC, ROWS, w), BF16),
            pltpu.VMEM((n, 2 * hid, w), BF16),
            pltpu.VMEM((n, hid, w), BF16),
            dma((2,)), dma((2, 2)), dma((n,)), dma((n,)), dma((n,)), dma((n,)), dma((n,)), dma((n,)),
            dma((n, 7)), dma((n, 7)), dma((n,)), dma((n,)), dma((n, 3)),
        ],
        compiler_params=pltpu.CompilerParams(collective_id=1, has_side_effects=True, vmem_limit_bytes=VMEM_LIMIT),
    )(act, act_t, st, w_gate[0], w_up[0], rows)
    return (d_tok, d_gate[None], d_up[None], d_down[None])


def solution(mesh):
    rows = P(("dp", "expert"), None)
    weights = P("expert", "dp", None)
    return jax.shard_map(
        per_device,
        mesh=mesh,
        in_specs=(rows, rows, rows, rows, weights, weights, weights),
        out_specs=(rows, weights, weights, weights),
        check_vma=False,
    )
```

```python
import jax
import jax.numpy as jnp
from jax import lax
from jax.experimental import pallas as pl
from jax.experimental.pallas import tpu as pltpu
from jax.sharding import PartitionSpec as P

MESH = pl.DeviceIdType.MESH
F32, BF16 = jnp.float32, jnp.bfloat16
VMEM_LIMIT = 67043328

NY, NX, NZ, NCORE = 4, 4, 8, 2
CAP = 4
TOK = 24
PAD = 32
SRC = NX * NCORE
ROWS = NZ * CAP
LAG, LATE_LAG = 2, 3
RLAG, RLATE_LAG = 2, 2
WIDTH = 256


class Place:
    def __init__(self):
        self.y = lax.axis_index("dp")
        e = lax.axis_index("expert")
        self.c = lax.rem(e, NCORE)
        self.z = lax.rem(lax.div(e, NCORE), NZ)
        self.x = lax.div(e, NCORE * NZ)

    @staticmethod
    def first(i):
        return i + 1 - 2 * lax.rem(i, 2)

    @staticmethod
    def second(i):
        return 3 - i

    def pick(self, i, s):
        return (1 - s) * self.first(i) + s * self.second(i)

    def at(self, y=None, x=None, z=None, c=None):
        y = self.y if y is None else y
        x = self.x if x is None else x
        z = self.z if z is None else z
        c = self.c if c is None else c
        return (y, (x * NZ + z) * NCORE + c)

    def zz(self, d):
        return lax.rem(self.z + d + NZ, NZ)

    def enter(self):
        sem = pltpu.get_barrier_semaphore()
        peers = [self.at(y=self.first(self.y)), self.at(y=self.second(self.y))]
        peers += [self.at(z=self.zz(1)), self.at(z=self.zz(-1)), self.at(c=1 - self.c)]
        for x in (self.first(self.x), self.second(self.x)):
            peers += [self.at(x=x, c=0), self.at(x=x, c=1)]
        for p in peers:
            pl.semaphore_signal(sem, inc=1, device_id=p, device_id_type=MESH)
        pl.semaphore_wait(sem, len(peers))


def send(src, dst, ssem, rsem, device):
    pltpu.make_async_remote_copy(
        src_ref=src, dst_ref=dst, send_sem=ssem, recv_sem=rsem, device_id=device, device_id_type=MESH
    ).start()


def await_(ref, sem):
    pltpu.make_async_copy(ref, ref, sem).wait()


def when(i, n):
    return pl.when(jnp.logical_and(i >= 0, i < n))


def dot(a, b, dims=((1,), (0,))):
    return lax.dot_general(a, b, (dims, ((), ())), preferred_element_type=F32)


def slot_exchange(p, s, i, sel, fwd, into, send_sem, fwd_send, fwd_recv, recv_sem):
    mine = p.c
    send(sel.at[i, :, 1 - mine], into.at[:, mine], send_sem, recv_sem, p.at(c=1 - mine))
    send(sel.at[i, :, pl.ds(6, 2)], fwd.at[i], send_sem, fwd_recv, p.at(x=p.pick(p.x, s)))
    for d, x in ((1, p.first(p.x)), (2, p.second(p.x))):
        for c in range(NCORE):
            send(sel.at[i, :, d * 2 + c], into.at[:, d * 2 + mine], send_sem, recv_sem, p.at(x=x, c=c))


def pass_on(p, s, i, fwd, into, fwd_send, recv_sem):
    for c in range(NCORE):
        send(fwd.at[i, :, c], into.at[:, 6 + p.c], fwd_send, recv_sem, p.at(x=p.pick(p.x, 1 - s), c=c))


def quarter(pos, s):
    return (0, 1 + s, 2 - s, 3)[pos]


def route_stage(tok, info, wg, wu, wd, rows_out, act_t_out, act_out, st_out,
                zbuf, sel, fwd, rows, wgu, wdn, acc_gu, acc_d, sm, rb,
                sem_l, a_s, a_r, z_s, z_r, x_s, x_r, f_s, f_r, l_s, l_r, o_s, r_s, r_r):
    p = Place()
    n, _, w = tok.shape
    half = n // 2
    hid = wg.shape[0]
    y1, y2 = p.first(p.y), p.second(p.y)

    own_tok = pltpu.make_async_copy(tok, zbuf.at[:, 0, p.z], sem_l.at[0])
    own_tok.start()
    own_info = pltpu.make_async_copy(info, rb.at[0, p.z], sem_l.at[1])
    own_info.start()
    loads = [
        pltpu.make_async_copy(wg, wgu.at[pl.ds(0, hid)], sem_l.at[2]),
        pltpu.make_async_copy(wu, wgu.at[pl.ds(hid, hid)], sem_l.at[3]),
        pltpu.make_async_copy(wd, wdn, sem_l.at[4]),
    ]
    for cp in loads:
        cp.start()
    p.enter()
    send(info, rb.at[1, p.z], r_s.at[7], r_r.at[7], p.at(y=y1))
    send(info, rb.at[2, p.z], r_s.at[8], r_r.at[8], p.at(y=y2))

    @pl.loop(0, n)
    def _(i):
        send(tok.at[i], zbuf.at[i, 1, p.z], a_s.at[i], a_r.at[i], p.at(y=p.pick(p.y, lax.rem(i, 2))))

    acc_gu[...] = jnp.zeros_like(acc_gu)
    acc_d[...] = jnp.zeros_like(acc_d)

    def z_hop(buf, k, ssem, rsem):
        for side, d in ((0, 1), (1, -1)):
            block = p.zz(-d * (k - 1))
            send(buf.at[:, block], buf.at[:, block], ssem(2 * (k - 1) + side), rsem.at[2 * (k - 1) + side], p.at(z=p.zz(d)))

    def z_last(buf, s, ssem, rsem):
        d = 1 - 2 * s
        block = p.zz(-3 * d)
        send(buf.at[:, block], buf.at[:, block], ssem(6), rsem.at[6], p.at(z=p.zz(d)))

    def z_wait(buf, k, rsem):
        for side in (0, 1):
            await_(buf.at[:, 0], rsem.at[2 * (k - 1) + side])

    def info_step(t):
        one = lambda j: r_s.at[j]

        @pl.when(t == 0)
        def _():
            own_info.wait()
            await_(info, r_r.at[7])
            await_(info, r_r.at[8])
            z_hop(rb, 1, one, r_r)

        for k in (1, 2):

            @pl.when(t == k * LAG)
            def _(k=k):
                z_wait(rb, k, r_r)
                z_hop(rb, k + 1, one, r_r)

        @pl.when(t == 3 * LAG)
        def _():
            z_wait(rb, 3, r_r)
            z_last(rb, 0, one, r_r)

        @pl.when(t == 4 * LAG)
        def _():
            await_(rb.at[:, 0], r_r.at[6])
            select_matrices()

    def select_matrices():
        lane = lax.broadcasted_iota(jnp.int32, (128, 128), 1)
        sub = lax.broadcasted_iota(jnp.int32, (128, 128), 0)
        before = jnp.where(jnp.logical_and(sub < lane, lax.div(sub, PAD) == lax.div(lane, PAD)), 1.0, 0.0).astype(BF16)
        r_row = lax.broadcasted_iota(jnp.int32, (ROWS, 128), 0)
        r_lane = lax.broadcasted_iota(jnp.int32, (ROWS, 128), 1)
        row_z, row_slot = lax.div(r_row, CAP), lax.rem(r_row, CAP).astype(F32)
        xs = (p.x, p.first(p.x), p.second(p.x), lax.rem(p.x + 2, NX))
        for role in range(3):
            for zh in range(2):
                both = rb[role, 4 * zh].astype(F32)
                for q in range(1, 4):
                    both = both + rb[role, 4 * zh + q].astype(F32)
                route, gate = both[0:8].astype(jnp.int32), both[8:16]
                chosen, value = [], []
                for d in range(4):
                    for c in range(NCORE):
                        hit = route == (xs[d] * NZ + p.z) * NCORE + c + 1
                        chosen.append(jnp.sum(jnp.where(hit, 1.0, 0.0), axis=0, keepdims=True))
                        value.append(jnp.sum(jnp.where(hit, gate, 0.0), axis=0, keepdims=True))
                chosen = jnp.concatenate(chosen, axis=0)
                earlier = dot(chosen.astype(BF16), before)
                same_z = row_z == 4 * zh + lax.div(r_lane, PAD)
                for e in range(SRC):
                    spread = lambda v: jnp.broadcast_to(v, (ROWS, 128))
                    hit = jnp.logical_and(same_z, jnp.logical_and(spread(chosen[e : e + 1]) > 0.5, spread(earlier[e : e + 1]) == row_slot))
                    place = (pl.ds(e * ROWS, ROWS), pl.ds(zh * 128, 128))
                    sm[0, role, place[0], place[1]] = jnp.where(hit, 1.0, 0.0).astype(BF16)
                    sm[1, role, place[0], place[1]] = jnp.where(hit, spread(value[e]), 0.0).astype(BF16)
            st_out[role] = sm[0, role].astype(F32).T.astype(BF16)

    def step(t, carry):
        i6, i5, i4, i3, i2, i1 = (t - k * LAG for k in (6, 5, 4, 3, 2, 1))

        @when(i6, n)
        def _():
            await_(rows.at[i6, 0, :, pl.ds(0, 7)], x_r.at[i6])
            late = p.at(y=p.pick(p.y, 1 - lax.rem(i6, 2)))
            send(rows.at[i6, 0], rows.at[i6, 1], l_s.at[i6], l_r.at[i6], late)

        @when(i5, n)
        def _():
            await_(fwd.at[i5], f_r.at[i5])
            pass_on(p, lax.rem(i5, 2), i5, fwd, rows.at[i5, 0], f_s.at[i5], x_r.at[i5])

        info_step(t)

        @when(i4, n)
        def _():
            s = lax.rem(i4, 2)
            which = lax.div(i4, half)
            await_(zbuf.at[i4, :, 0], z_r.at[i4, 6])
            for ys, role in ((0, 0), (1, 1 + s)):
                got = dot(sm[which, role], zbuf[i4, ys].reshape(NZ * PAD, w)).astype(BF16)
                sel[i4, ys] = got.reshape(SRC, ROWS, w)
            rows[i4, 0, :, p.c] = sel[i4, :, p.c]
            slot_exchange(p, s, i4, sel, fwd, rows.at[i4, 0], x_s.at[i4], f_s.at[i4], f_r.at[i4], x_r.at[i4])

        @when(i3, n)
        def _():
            z_wait(zbuf.at[i3], 3, z_r.at[i3])
            z_last(zbuf.at[i3], lax.rem(i3, 2), lambda j: z_s.at[i3], z_r.at[i3])

        for i, k in ((i2, 2), (i1, 1)):

            @when(i, n)
            def _(i=i, k=k):
                z_wait(zbuf.at[i], k, z_r.at[i])
                z_hop(zbuf.at[i], k + 1, lambda j: z_s.at[i], z_r.at[i])

        @when(t, n)
        def _():
            @pl.when(t == 0)
            def _():
                own_tok.wait()

            await_(tok.at[t], a_r.at[t])
            z_hop(zbuf.at[t], 1, lambda j: z_s.at[t], z_r.at[t])

        i8 = t - 6 * LAG - LATE_LAG

        @pl.when(i8 == 0)
        def _():
            for cp in loads:
                cp.wait()

        @when(i8, n)
        def _():
            s = lax.rem(i8, 2)
            await_(rows.at[i8, 1], l_r.at[i8])
            for h in range(2):
                for ys in range(2):
                    k = pl.multiple_of((2 * h + ys) * SRC * ROWS, SRC * ROWS)
                    pltpu.make_async_copy(rows.at[i8, h, ys], rows_out.at[i8, 2 * h + ys], o_s.at[i8, 2 * h + ys]).start()

            def multiply(acc, weights):
                j = lax.rem(i8, half)
                cols = weights[:, pl.ds(pl.multiple_of(j * w, w), w)]
                for h in range(2):
                    for ys in range(2):
                        q = quarter(2 * h + ys, s)
                        at = pl.ds(pl.multiple_of(q * SRC * ROWS, SRC * ROWS), SRC * ROWS)
                        acc[:, at] += dot(cols, rows[i8, h, ys].reshape(SRC * ROWS, w), ((1,), (1,)))

            @pl.when(i8 < half)
            def _():
                multiply(acc_gu, wgu)

            @pl.when(i8 >= half)
            def _():
                multiply(acc_d, wdn)

        return carry

    lax.fori_loop(0, n + 6 * LAG + LATE_LAG, step, 0)

    for q in range(4):
        at = pl.ds(q * SRC * ROWS, SRC * ROWS)
        gate_pre, up_pre, d_hidden = acc_gu[0:hid, at], acc_gu[hid : 2 * hid, at], acc_d[:, at]
        sig = jax.nn.sigmoid(gate_pre)
        silu = gate_pre * sig
        d_up = d_hidden * silu
        d_gate = d_hidden * up_pre * sig * (1.0 + gate_pre * (1.0 - sig))
        both = jnp.concatenate([d_gate, d_up], axis=0)
        act_t_out[0 : 2 * hid, at] = both.astype(BF16)
        act_t_out[2 * hid : 3 * hid, at] = (silu * up_pre).astype(BF16)
        act_out[at, :] = both.T.astype(BF16)

    @pl.loop(0, n)
    def _(i):
        await_(tok.at[i], a_s.at[i])
        await_(zbuf.at[i, :, pl.ds(0, 7)], z_s.at[i])
        await_(sel.at[i, :, pl.ds(0, 7)], x_s.at[i])
        await_(fwd.at[i], f_s.at[i])
        await_(rows.at[i, 0], l_s.at[i])
        for k in range(4):
            await_(rows.at[i, 0, 0], o_s.at[i, k])

    for j in range(7):
        await_(rb.at[:, 0], r_s.at[j])
    await_(info, r_s.at[7])
    await_(info, r_s.at[8])


def return_stage(act, act_t, st, wg, wu, rows_in, d_tok, d_gate, d_up, d_down,
                 wgu, acts, keep, part, got, total, fwd, back, own, zs, zr, tail, tail_in, xr, gr, dw_gu, dw_d,
                 sem_l, in_s, l_s, l_r, x_s, x_r, f_s, f_r, z_s, z_r, e_s, e_r, o_s):
    p = Place()
    n, w = keep.shape[0], keep.shape[-1]
    hid = wg.shape[0]
    qr = SRC * ROWS

    loads = [
        pltpu.make_async_copy(wg, wgu.at[pl.ds(0, hid)], sem_l.at[0]),
        pltpu.make_async_copy(wu, wgu.at[pl.ds(hid, hid)], sem_l.at[1]),
    ]
    for cp in loads:
        cp.start()

    def fetch(i, slot):
        pltpu.make_async_copy(rows_in.at[i], xr.at[slot], in_s.at[slot, 0]).start()
        pltpu.make_async_copy(rows_in.at[n + i], gr.at[slot], in_s.at[slot, 1]).start()

    fetch(0, 0)
    p.enter()
    acts[0] = act_t[...]
    for pos in range(4):
        acts[1, :, pl.ds(pos * qr, qr)] = act_t[:, pl.ds(quarter(pos, 1) * qr, qr)]
    for cp in loads:
        cp.wait()

    def z_send(i, k, side, src):
        j = 6 if k == 4 else 2 * (k - 1) + side
        d = 2 * side - 1
        send(src, zr.at[i, j], z_s.at[i, j], z_r.at[i, j], p.at(z=p.zz(d)))

    def step(t, carry):
        i1, i2, i3, i4, i5, i6, i7, i8 = (t - RLATE_LAG - k * RLAG for k in range(8))
        m = t - RLATE_LAG

        @when(t, n)
        def _():
            s = lax.rem(t, 2)
            cols = wgu[:, pl.ds(pl.multiple_of(t * w, w), w)]
            for pos in (2, 3, 0, 1):
                q = quarter(pos, s)
                a = act[pl.ds(pl.multiple_of(q * qr, qr), qr), :]
                value = dot(a, cols).astype(BF16).reshape(SRC, ROWS, w)
                if pos >= 2:
                    part[t, pos - 2] = value
                else:
                    keep[t, pos] = value
                if pos == 3:
                    late = p.at(y=p.pick(p.y, 1 - s))
                    send(part.at[t], got.at[t], l_s.at[t], l_r.at[t], late)

        @when(i1, n)
        def _():
            s = lax.rem(i1, 2)
            await_(got.at[i1], l_r.at[i1])
            total[i1] = (keep[i1].astype(F32) + got[i1].astype(F32)).astype(BF16)
            back[i1, :, p.c] = total[i1, :, p.c]
            slot_exchange(p, s, i1, total, fwd, back.at[i1], x_s.at[i1], f_s.at[i1], f_r.at[i1], x_r.at[i1])

        @when(i2, n)
        def _():
            await_(fwd.at[i2], f_r.at[i2])
            pass_on(p, lax.rem(i2, 2), i2, fwd, back.at[i2], f_s.at[i2], x_r.at[i2])

        @when(i3, n)
        def _():
            s = lax.rem(i3, 2)
            await_(back.at[i3, :, pl.ds(0, 7)], x_r.at[i3])
            for ys, role in ((0, 0), (1, 1 + s)):
                value = dot(st[role], back[i3, ys].reshape(qr, w)).astype(BF16)
                own[i3, ys] = value.reshape(NZ, PAD, w)
            block = own.at[i3, :, p.zz(4)]
            d = 2 * s - 1
            send(block, zr.at[i3, 6], z_s.at[i3, 6], z_r.at[i3, 6], p.at(z=p.zz(d)))

        @when(i4, n)
        def _():
            s = lax.rem(i4, 2)
            await_(zr.at[i4, 6], z_r.at[i4, 6])
            four = zr[i4, 6].astype(F32)
            for side in (0, 1):
                mine = own[i4, :, p.zz(3 * (2 * side - 1))].astype(F32)
                add = four * jnp.where(s == side, 1.0, 0.0)
                zs[i4, 4 + side] = (mine + add).astype(BF16)
                z_send(i4, 3, side, zs.at[i4, 4 + side])

        for i, k in ((i5, 2), (i6, 1)):

            @when(i, n)
            def _(i=i, k=k):
                for side in (0, 1):
                    await_(zr.at[i, 0], z_r.at[i, 2 * k + side])
                    mine = own[i, :, p.zz(k * (2 * side - 1))].astype(F32)
                    j = 2 * (k - 1) + side
                    zs[i, j] = (mine + zr[i, 2 * k + side].astype(F32)).astype(BF16)
                    z_send(i, k, side, zs.at[i, j])

        @when(i7, n)
        def _():
            for side in (0, 1):
                await_(zr.at[i7, 0], z_r.at[i7, side])
            value = own[i7, :, p.z].astype(F32) + zr[i7, 0].astype(F32) + zr[i7, 1].astype(F32)
            zs[i7, 6, 0] = value[0].astype(BF16)
            tail[i7] = value[1].astype(BF16)
            send(tail.at[i7], tail_in.at[i7], e_s.at[i7], e_r.at[i7], p.at(y=p.pick(p.y, lax.rem(i7, 2))))

        @when(i8, n)
        def _():
            await_(tail_in.at[i8], e_r.at[i8])
            value = zs[i8, 6, 0].astype(F32) + tail_in[i8].astype(F32)
            d_tok[:, pl.ds(pl.multiple_of(i8 * w, w), w)] = value[0:TOK].astype(BF16)

        @when(m, n)
        def _():
            slot = lax.rem(m, 2)

            @pl.when(m + 1 < n)
            def _():
                fetch(m + 1, 1 - slot)

            await_(xr.at[slot], in_s.at[slot, 0])
            await_(gr.at[slot], in_s.at[slot, 1])
            a = acts[slot]
            x_all = xr[slot].reshape(4 * qr, w)
            g_all = gr[slot].reshape(4 * qr, w)
            dw_gu[m] = dot(a[0 : 2 * hid], x_all).astype(BF16)
            dw_d[m] = dot(a[2 * hid : 3 * hid], g_all).astype(BF16)
            at = pl.ds(pl.multiple_of(m * w, w), w)
            pltpu.make_async_copy(dw_gu.at[m, pl.ds(0, hid)], d_gate.at[:, at], o_s.at[m, 0]).start()
            pltpu.make_async_copy(dw_gu.at[m, pl.ds(hid, hid)], d_up.at[:, at], o_s.at[m, 1]).start()
            pltpu.make_async_copy(dw_d.at[m], d_down.at[:, at], o_s.at[m, 2]).start()

        return carry

    lax.fori_loop(0, n + RLATE_LAG + 7 * RLAG, step, 0)

    @pl.loop(0, n)
    def _(i):
        await_(part.at[i], l_s.at[i])
        await_(total.at[i, :, pl.ds(0, 7)], x_s.at[i])
        await_(fwd.at[i], f_s.at[i])
        for j in range(7):
            await_(zr.at[i, j], z_s.at[i, j])
        await_(tail.at[i], e_s.at[i])
        for j in range(3):
            await_(dw_d.at[i], o_s.at[i, j])


def per_device(tokens, out_grad, routes, gates, w_gate, w_up, w_down):
    width = tokens.shape[1]
    w = WIDTH
    nc = width // w
    n = 2 * nc
    hid = w_gate.shape[1]
    qr = SRC * ROWS
    z = lax.rem(lax.div(lax.axis_index("expert"), NCORE), NZ)

    def chunks(a):
        a = jnp.pad(a, ((0, PAD - TOK), (0, 0)))
        return a.reshape(PAD, nc, w).transpose(1, 0, 2)

    tok = jnp.concatenate([chunks(tokens), chunks(out_grad)], axis=0)
    info = jnp.concatenate([(routes + 1).astype(BF16).T, gates.T], axis=0)
    info = jnp.pad(info, ((0, 0), (0, PAD - TOK)))
    info = jnp.where(lax.broadcasted_iota(jnp.int32, (16, 4, PAD), 1) == lax.rem(z, 4), info[:, None, :], 0).reshape(16, 128)

    anywhere = pl.BlockSpec(memory_space=pl.ANY)
    vmem = pl.BlockSpec(memory_space=pltpu.VMEM)
    dma = pltpu.SemaphoreType.DMA
    shape = jax.ShapeDtypeStruct
    rows, act_t, act, st = pl.pallas_call(
        route_stage,
        out_shape=(shape((n, 4, SRC, ROWS, w), BF16), shape((3 * hid, 4 * qr), BF16), shape((4 * qr, 2 * hid), BF16), shape((3, qr, qr), BF16)),
        in_specs=[anywhere, vmem, anywhere, anywhere, anywhere],
        out_specs=(anywhere, vmem, vmem, vmem),
        scratch_shapes=[
            pltpu.VMEM((n, 2, NZ, PAD, w), BF16),
            pltpu.VMEM((n, 2, SRC, ROWS, w), BF16),
            pltpu.VMEM((n, 2, 2, ROWS, w), BF16),
            pltpu.VMEM((n, 2, 2, SRC, ROWS, w), BF16),
            pltpu.VMEM((2 * hid, width), BF16),
            pltpu.VMEM((hid, width), BF16),
            pltpu.VMEM((2 * hid, 4 * qr), F32),
            pltpu.VMEM((hid, 4 * qr), F32),
            pltpu.VMEM((2, 3, qr, qr), BF16),
            pltpu.VMEM((3, NZ, 16, 128), BF16),
            dma((5,)), dma((n,)), dma((n,)), dma((n,)), dma((n, 7)), dma((n,)), dma((n,)), dma((n,)), dma((n,)),
            dma((n,)), dma((n,)), dma((n, 4)), dma((9,)), dma((9,)),
        ],
        compiler_params=pltpu.CompilerParams(collective_id=0, has_side_effects=True, vmem_limit_bytes=VMEM_LIMIT),
    )(tok, info, w_gate[0], w_up[0], w_down[0])

    n = nc
    d_tok, d_gate, d_up, d_down = pl.pallas_call(
        return_stage,
        out_shape=(shape((TOK, width), BF16),) + (shape((hid, width), BF16),) * 3,
        in_specs=[vmem, vmem, vmem, anywhere, anywhere, anywhere],
        out_specs=(vmem, anywhere, anywhere, anywhere),
        scratch_shapes=[
            pltpu.VMEM((2 * hid, width), BF16),
            pltpu.VMEM((2, 3 * hid, 4 * qr), BF16),
            pltpu.VMEM((n, 2, SRC, ROWS, w), BF16),
            pltpu.VMEM((n, 2, SRC, ROWS, w), BF16),
            pltpu.VMEM((n, 2, SRC, ROWS, w), BF16),
            pltpu.VMEM((n, 2, SRC, ROWS, w), BF16),
            pltpu.VMEM((n, 2, 2, ROWS, w), BF16),
            pltpu.VMEM((n, 2, SRC, ROWS, w), BF16),
            pltpu.VMEM((n, 2, NZ, PAD, w), BF16),
            pltpu.VMEM((n, 7, 2, PAD, w), BF16),
            pltpu.VMEM((n, 7, 2, PAD, w), BF16),
            pltpu.VMEM((n, PAD, w), BF16),
            pltpu.VMEM((n, PAD, w), BF16),
            pltpu.VMEM((2, 4, SRC, ROWS, w), BF16),
            pltpu.VMEM((2, 4, SRC, ROWS, w), BF16),
            pltpu.VMEM((n, 2 * hid, w), BF16),
            pltpu.VMEM((n, hid, w), BF16),
            dma((2,)), dma((2, 2)), dma((n,)), dma((n,)), dma((n,)), dma((n,)), dma((n,)), dma((n,)),
            dma((n, 7)), dma((n, 7)), dma((n,)), dma((n,)), dma((n, 3)),
        ],
        compiler_params=pltpu.CompilerParams(collective_id=1, has_side_effects=True, vmem_limit_bytes=VMEM_LIMIT),
    )(act, act_t, st, w_gate[0], w_up[0], rows)
    return (d_tok, d_gate[None], d_up[None], d_down[None])


def solution(mesh):
    rows = P(("dp", "expert"), None)
    weights = P("expert", "dp", None)
    return jax.shard_map(
        per_device,
        mesh=mesh,
        in_specs=(rows, rows, rows, rows, weights, weights, weights),
        out_specs=(rows, weights, weights, weights),
        check_vma=False,
    )
```

```python
import jax
import jax.numpy as jnp
from jax import lax
from jax.experimental import pallas as pl
from jax.experimental.pallas import tpu as pltpu
from jax.sharding import PartitionSpec as P

MESH = pl.DeviceIdType.MESH
F32, BF16 = jnp.float32, jnp.bfloat16
VMEM_LIMIT = 67043328

NY, NX, NZ, NCORE = 4, 4, 8, 2
CAP = 4
TOK = 24
PAD = 32
SRC = NX * NCORE
ROWS = NZ * CAP
QUARTER = SRC * ROWS
WIDTH = 256
LAG, LATE_LAG = 2, 5
RLATE_LAG, RLAG = 4, 2
DW_LAG = 2
REAL = pl.ds(0, TOK)


class Place:
    def __init__(self):
        self.y = lax.axis_index("dp")
        e = lax.axis_index("expert")
        self.c = lax.rem(e, NCORE)
        self.z = lax.rem(lax.div(e, NCORE), NZ)
        self.x = lax.div(e, NCORE * NZ)

    @staticmethod
    def first(i):
        return i + 1 - 2 * lax.rem(i, 2)

    @staticmethod
    def second(i):
        return 3 - i

    def pick(self, i, s):
        return (1 - s) * self.first(i) + s * self.second(i)

    def at(self, y=None, x=None, z=None, c=None):
        y = self.y if y is None else y
        x = self.x if x is None else x
        z = self.z if z is None else z
        c = self.c if c is None else c
        return (y, (x * NZ + z) * NCORE + c)

    def zz(self, d):
        return lax.rem(self.z + d + NZ, NZ)

    def enter(self):
        sem = pltpu.get_barrier_semaphore()
        peers = [self.at(y=self.first(self.y)), self.at(y=self.second(self.y)), self.at(c=1 - self.c)]
        peers += [self.at(z=self.zz(d)) for d in (1, -1, 2, -2)]
        for x in (self.first(self.x), self.second(self.x)):
            peers += [self.at(x=x, c=0), self.at(x=x, c=1)]
        for p in peers:
            pl.semaphore_signal(sem, inc=1, device_id=p, device_id_type=MESH)
        pl.semaphore_wait(sem, len(peers))


def send(src, dst, ssem, rsem, device):
    pltpu.make_async_remote_copy(
        src_ref=src, dst_ref=dst, send_sem=ssem, recv_sem=rsem, device_id=device, device_id_type=MESH
    ).start()


def await_(ref, sem):
    pltpu.make_async_copy(ref, ref, sem).wait()


def when(i, n):
    return pl.when(jnp.logical_and(i >= 0, i < n))


def dot(a, b, dims=((1,), (0,))):
    return lax.dot_general(a, b, (dims, ((), ())), preferred_element_type=F32)


def slot_exchange(p, s, sel, fwd, into, send_sem, fwd_recv, recv_sem):
    mine = p.c
    send(sel.at[:, pl.ds(6, 2)], fwd, send_sem, fwd_recv, p.at(x=p.pick(p.x, s)))
    for d, x in ((1, p.first(p.x)), (2, p.second(p.x))):
        for c in range(NCORE):
            send(sel.at[:, d * 2 + c], into.at[:, d * 2 + mine], send_sem, recv_sem, p.at(x=x, c=c))
    send(sel.at[:, 1 - mine], into.at[:, mine], send_sem, recv_sem, p.at(c=1 - mine))


def pass_on(p, s, fwd, into, fwd_send, recv_sem):
    for c in range(NCORE):
        send(fwd.at[:, c], into.at[:, 6 + p.c], fwd_send, recv_sem, p.at(x=p.pick(p.x, 1 - s), c=c))


def gather_near(p, block, ssem, rsem):
    mine = block(p.z)
    for j, d in enumerate((2, -2, 1, -1)):
        send(mine, mine, ssem(j), rsem.at[j], p.at(z=p.zz(d)))


def gather_far(p, s, block, ssem, rsem):
    for j in (0, 1):
        await_(block(p.z), rsem.at[j])
    d = 2 - 4 * s
    far = block(p.zz(-d))
    send(far, far, ssem(6), rsem.at[6], p.at(z=p.zz(d)))
    for j, d in enumerate((1, -1)):
        passed = block(p.zz(-2 * d))
        send(passed, passed, ssem(4 + j), rsem.at[4 + j], p.at(z=p.zz(d)))


def gather_wait(p, block, rsem):
    for j in range(2, 7):
        await_(block(p.z), rsem.at[j])


def quarter(pos, s):
    return (0, 1 + s, 2 - s, 3)[pos]


def select_matrices(p, rb, sm, st):
    lane = lax.broadcasted_iota(jnp.int32, (128, 128), 1)
    sub = lax.broadcasted_iota(jnp.int32, (128, 128), 0)
    before = jnp.where(jnp.logical_and(sub < lane, lax.div(sub, PAD) == lax.div(lane, PAD)), 1.0, 0.0).astype(BF16)
    r_row = lax.broadcasted_iota(jnp.int32, (ROWS, 128), 0)
    r_lane = lax.broadcasted_iota(jnp.int32, (ROWS, 128), 1)
    row_z, row_slot = lax.div(r_row, CAP), lax.rem(r_row, CAP).astype(F32)
    xs = (p.x, p.first(p.x), p.second(p.x), lax.rem(p.x + 2, NX))
    spread = lambda v: jnp.broadcast_to(v, (ROWS, 128))
    for role in range(3):
        for zh in range(2):
            both = rb[role, 4 * zh].astype(F32)
            for q in range(1, 4):
                both = both + rb[role, 4 * zh + q].astype(F32)
            route, gate = both[0:8].astype(jnp.int32), both[8:16]
            chosen, value = [], []
            for d in range(4):
                for c in range(NCORE):
                    hit = route == (xs[d] * NZ + p.z) * NCORE + c + 1
                    chosen.append(jnp.sum(jnp.where(hit, 1.0, 0.0), axis=0, keepdims=True))
                    value.append(jnp.sum(jnp.where(hit, gate, 0.0), axis=0, keepdims=True))
            chosen = jnp.concatenate(chosen, axis=0)
            earlier = dot(chosen.astype(BF16), before)
            same_z = row_z == 4 * zh + lax.div(r_lane, PAD)
            for e in range(SRC):
                hit = jnp.logical_and(spread(chosen[e : e + 1]) > 0.5, spread(earlier[e : e + 1]) == row_slot)
                hit = jnp.logical_and(same_z, hit)
                rows, cols = pl.ds(e * ROWS, ROWS), pl.ds(zh * 128, 128)
                sm[0, role, rows, cols] = jnp.where(hit, 1.0, 0.0).astype(BF16)
                sm[1, role, rows, cols] = jnp.where(hit, spread(value[e]), 0.0).astype(BF16)
        st[role] = sm[0, role].astype(F32).T.astype(BF16)


def layer(tok, ograd, info, wg, wu, wd, d_tok, d_gate, d_up, d_down,
          zbuf, sel, fwd, rows, wgu, wdn, acc_gu, acc_d, sm, st, rb, act_t, act,
          got, back, fwd2, zr, tail, tail_in, dw_gu, dw_d,
          sem_l, a_s, a_r, z_s, z_r, x_s, x_r, f_s, f_r, l_s, l_r, r_s, r_r,
          l2_s, l2_r, x2_s, x2_r, f2_s, f2_r, z2_s, z2_r, e_s, e_r, o_s):
    p = Place()
    n, w = zbuf.shape[0], zbuf.shape[-1]
    half = n // 2
    hid = wg.shape[0]
    qr = QUARTER

    def cols(i):
        return pl.ds(pl.multiple_of(i * w, w), w)

    own_info = pltpu.make_async_copy(info, rb.at[0, p.z], sem_l.at[0])
    own_info.start()
    for k, ref in enumerate((tok, ograd)):

        @pl.loop(0, half)
        def _(j, k=k, ref=ref):
            pltpu.make_async_copy(ref.at[:, cols(j)], zbuf.at[k * half + j, 0, p.z, REAL], sem_l.at[1 + k]).start()

    p.enter()
    send(info, rb.at[1, p.z], r_s.at[7], r_r.at[7], p.at(y=p.first(p.y)))
    send(info, rb.at[2, p.z], r_s.at[8], r_r.at[8], p.at(y=p.second(p.y)))
    for k, ref in enumerate((tok, ograd)):

        @pl.loop(0, half)
        def _(j, k=k, ref=ref):
            i = k * half + j
            to = p.at(y=p.pick(p.y, lax.rem(j, 2)))
            send(ref.at[:, cols(j)], zbuf.at[i, 1, p.z, REAL], a_s.at[i], a_r.at[i], to)

    loads = [
        pltpu.make_async_copy(wg, wgu.at[pl.ds(0, hid)], sem_l.at[3]),
        pltpu.make_async_copy(wu, wgu.at[pl.ds(hid, hid)], sem_l.at[4]),
        pltpu.make_async_copy(wd, wdn, sem_l.at[5]),
    ]
    for cp in loads:
        cp.start()

    zbuf[:, :, :, pl.ds(TOK, PAD - TOK), :] = jnp.zeros((n, 2, NZ, PAD - TOK, w), BF16)
    acc_gu[...] = jnp.zeros_like(acc_gu)
    acc_d[...] = jnp.zeros_like(acc_d)

    info_block = lambda z: rb.at[:, z]
    token_block = lambda i: lambda z: zbuf.at[i, :, z, REAL]

    def step(t, carry):
        i_far, i_sel, i_pass, i_late = (t - k * LAG for k in range(1, 5))
        i_mul = t - 4 * LAG - LATE_LAG

        @pl.when(t == 0)
        def _():
            own_info.wait()
            await_(info, r_r.at[7])
            await_(info, r_r.at[8])
            gather_near(p, info_block, lambda j: r_s.at[j], r_r)
            await_(tok, sem_l.at[1])

        @pl.when(t == LAG)
        def _():
            gather_far(p, 0, info_block, lambda j: r_s.at[j], r_r)

        @pl.when(t == 2 * LAG)
        def _():
            gather_wait(p, info_block, r_r)
            select_matrices(p, rb, sm, st)

        @when(t, n)
        def _():
            @pl.when(t == half)
            def _():
                await_(ograd, sem_l.at[2])

            await_(tok.at[:, pl.ds(0, w)], a_r.at[t])
            gather_near(p, token_block(t), lambda j: z_s.at[t], z_r.at[t])

        @when(i_far, n)
        def _():
            gather_far(p, lax.rem(i_far, 2), token_block(i_far), lambda j: z_s.at[i_far], z_r.at[i_far])

        @when(i_sel, n)
        def _():
            s = lax.rem(i_sel, 2)
            which = lax.div(i_sel, half)
            gather_wait(p, token_block(i_sel), z_r.at[i_sel])
            for ys, role in ((0, 0), (1, 1 + s)):
                chosen = dot(sm[which, role], zbuf[i_sel, ys].reshape(NZ * PAD, w)).astype(BF16)
                sel[i_sel, ys] = chosen.reshape(SRC, ROWS, w)
            slot_exchange(p, s, sel.at[i_sel], fwd.at[i_sel], rows.at[i_sel, 0], x_s.at[i_sel], f_r.at[i_sel], x_r.at[i_sel])
            rows[i_sel, 0, :, p.c] = sel[i_sel, :, p.c]

        @when(i_pass, n)
        def _():
            await_(fwd.at[i_pass], f_r.at[i_pass])
            pass_on(p, lax.rem(i_pass, 2), fwd.at[i_pass], rows.at[i_pass, 0], f_s.at[i_pass], x_r.at[i_pass])

        @when(i_late, n)
        def _():
            await_(rows.at[i_late, 0, :, pl.ds(0, 7)], x_r.at[i_late])
            late = p.at(y=p.pick(p.y, 1 - lax.rem(i_late, 2)))
            send(rows.at[i_late, 0], rows.at[i_late, 1], l_s.at[i_late], l_r.at[i_late], late)

        @pl.when(i_mul == 0)
        def _():
            for cp in loads:
                cp.wait()

        @when(i_mul, n)
        def _():
            s = lax.rem(i_mul, 2)
            await_(rows.at[i_mul, 1], l_r.at[i_mul])

            def multiply(acc, weights):
                part = weights[:, cols(lax.rem(i_mul, half))]
                for h in range(2):
                    for ys in range(2):
                        at = pl.ds(pl.multiple_of(quarter(2 * h + ys, s) * qr, qr), qr)
                        acc[:, at] += dot(part, rows[i_mul, h, ys].reshape(qr, w), ((1,), (1,)))

            @pl.when(i_mul < half)
            def _():
                multiply(acc_gu, wgu)

            @pl.when(i_mul >= half)
            def _():
                multiply(acc_d, wdn)

        return carry

    lax.fori_loop(0, n + 4 * LAG + LATE_LAG, step, 0)

    for q in range(4):
        at = pl.ds(q * qr, qr)
        swapped = pl.ds((0, 2, 1, 3)[q] * qr, qr)
        gate_pre, up_pre, d_hidden = acc_gu[0:hid, at], acc_gu[hid : 2 * hid, at], acc_d[:, at]
        sig = jax.nn.sigmoid(gate_pre)
        silu = gate_pre * sig
        d_up_act = d_hidden * silu
        d_gate_act = d_hidden * up_pre * sig * (1.0 + gate_pre * (1.0 - sig))
        both = jnp.concatenate([d_gate_act, d_up_act], axis=0)
        act[at, :] = both.T.astype(BF16)
        both, hidden = both.astype(BF16), (silu * up_pre).astype(BF16)
        for order, to in ((0, at), (1, swapped)):
            act_t[order, 0 : 2 * hid, to] = both
            act_t[order, 2 * hid : 3 * hid, to] = hidden

    @pl.loop(0, n)
    def _(i):
        await_(zbuf.at[i, :, pl.ds(0, 7), REAL], z_s.at[i])
        await_(sel.at[i, :, pl.ds(0, 7)], x_s.at[i])

    def part(i):
        return zbuf.at[i]

    def keep(i):
        return zbuf.at[half + i]

    def own(i):
        return sel.at[i]

    def sums(i):
        return sel.at[half + i]

    def back_step(t, carry):
        i_sum, i_pass, i_tok, i_far, i_end, i_out = (t - RLATE_LAG - k * RLAG for k in range(6))
        i_dw = t - DW_LAG

        @when(t, half)
        def _():
            s = lax.rem(t, 2)
            weights = wgu[:, cols(t)]
            for pos in (2, 3, 0, 1):
                a = act[pl.ds(pl.multiple_of(quarter(pos, s) * qr, qr), qr), :]
                value = dot(a, weights).astype(BF16).reshape(SRC, ROWS, w)
                if pos >= 2:
                    part(t)[pos - 2] = value
                else:
                    keep(t)[pos] = value
                if pos == 3:
                    send(part(t), got.at[t], l2_s.at[t], l2_r.at[t], p.at(y=p.pick(p.y, 1 - s)))

        @when(i_sum, half)
        def _():
            s = lax.rem(i_sum, 2)
            await_(got.at[i_sum], l2_r.at[i_sum])
            total = keep(i_sum)
            total[...] = (total[...].astype(F32) + got[i_sum].astype(F32)).astype(BF16)
            slot_exchange(p, s, total, fwd2.at[i_sum], back.at[i_sum], x2_s.at[i_sum], f2_r.at[i_sum], x2_r.at[i_sum])
            back[i_sum, :, p.c] = total[:, p.c]

        @when(i_pass, half)
        def _():
            await_(fwd2.at[i_pass], f2_r.at[i_pass])
            pass_on(p, lax.rem(i_pass, 2), fwd2.at[i_pass], back.at[i_pass], f2_s.at[i_pass], x2_r.at[i_pass])

        def z_send(i, j, src, d):
            send(src, zr.at[i, j], z2_s.at[i], z2_r.at[i, j], p.at(z=p.zz(d)))

        @when(i_tok, half)
        def _():
            s = lax.rem(i_tok, 2)
            await_(back.at[i_tok, :, pl.ds(0, 7)], x2_r.at[i_tok])
            mine = own(i_tok)
            for ys, role in ((0, 0), (1, 1 + s)):
                value = dot(st[role], back[i_tok, ys].reshape(qr, w)).astype(BF16)
                mine[ys] = value.reshape(NZ, PAD, w)
            d = 4 * s - 2
            z_send(i_tok, 2, mine.at[:, p.zz(4), REAL], d)
            for j, d in enumerate((-1, 1)):
                z_send(i_tok, j, mine.at[:, p.zz(3 * d), REAL], d)
                z_send(i_tok, 3 + j, mine.at[:, p.zz(d), REAL], d)

        @when(i_far, half)
        def _():
            s = lax.rem(i_far, 2)
            for j in range(3):
                await_(zr.at[i_far, j], z2_r.at[i_far, j])
            four = zr[i_far, 2].astype(F32)
            for j, d in enumerate((-2, 2)):
                value = own(i_far)[:, p.zz(d), REAL].astype(F32) + zr[i_far, j].astype(F32)
                value = value + jnp.where(s == j, four, 0.0)
                sums(i_far)[:, j, REAL] = value.astype(BF16)
                z_send(i_far, 5 + j, sums(i_far).at[:, j, REAL], d)

        @when(i_end, half)
        def _():
            for j in range(3, 7):
                await_(zr.at[i_end, j], z2_r.at[i_end, j])
            value = own(i_end)[:, p.z, REAL].astype(F32)
            for j in range(3, 7):
                value = value + zr[i_end, j].astype(F32)
            tail[i_end] = value.astype(BF16)
            send(tail.at[i_end, 1], tail_in.at[i_end], e_s.at[i_end], e_r.at[i_end], p.at(y=p.pick(p.y, lax.rem(i_end, 2))))

        @when(i_out, half)
        def _():
            await_(tail_in.at[i_out], e_r.at[i_out])
            value = tail[i_out, 0].astype(F32) + tail_in[i_out].astype(F32)
            d_tok[:, cols(i_out)] = value.astype(BF16)

        @when(i_dw, half)
        def _():
            slot = lax.rem(i_dw, 2)
            at = cols(i_dw)
            copies = (
                pltpu.make_async_copy(dw_gu.at[slot, pl.ds(0, hid)], d_gate.at[:, at], o_s.at[slot, 0]),
                pltpu.make_async_copy(dw_gu.at[slot, pl.ds(hid, hid)], d_up.at[:, at], o_s.at[slot, 1]),
                pltpu.make_async_copy(dw_d.at[slot], d_down.at[:, at], o_s.at[slot, 2]),
            )

            @pl.when(i_dw >= 2)
            def _():
                for cp in copies:
                    cp.wait()

            a = act_t.at[slot]
            dw_gu[slot] = dot(a[0 : 2 * hid], rows[i_dw].reshape(4 * qr, w)).astype(BF16)
            dw_d[slot] = dot(a[2 * hid : 3 * hid], rows[half + i_dw].reshape(4 * qr, w)).astype(BF16)
            for cp in copies:
                cp.start()

        return carry

    lax.fori_loop(0, half + RLATE_LAG + 5 * RLAG, back_step, 0)

    @pl.loop(0, n)
    def _(i):
        await_(tok.at[:, pl.ds(0, w)], a_s.at[i])
        await_(fwd.at[i], f_s.at[i])
        await_(rows.at[i, 0], l_s.at[i])

    @pl.loop(0, half)
    def _(i):
        await_(part(i), l2_s.at[i])
        await_(back.at[i, :, pl.ds(0, 7)], x2_s.at[i])
        await_(fwd2.at[i], f2_s.at[i])
        await_(zr.at[i], z2_s.at[i])
        await_(tail_in.at[i], e_s.at[i])

    for slot in range(2):
        for j in range(3):
            await_(dw_d.at[slot], o_s.at[slot, j])
    for j in range(7):
        await_(rb.at[:, 0], r_s.at[j])
    await_(info, r_s.at[7])
    await_(info, r_s.at[8])


def per_device(tokens, out_grad, routes, gates, w_gate, w_up, w_down):
    width = tokens.shape[1]
    w = WIDTH
    half = width // w
    n = 2 * half
    hid = w_gate.shape[1]
    qr = QUARTER
    z = lax.rem(lax.div(lax.axis_index("expert"), NCORE), NZ)

    info = jnp.concatenate([(routes + 1).astype(BF16).T, gates.T], axis=0)
    info = jnp.pad(info, ((0, 0), (0, PAD - TOK)))
    info = jnp.where(lax.broadcasted_iota(jnp.int32, (16, 4, PAD), 1) == lax.rem(z, 4), info[:, None, :], 0).reshape(16, 128)

    anywhere = pl.BlockSpec(memory_space=pl.ANY)
    vmem = pl.BlockSpec(memory_space=pltpu.VMEM)
    dma = pltpu.SemaphoreType.DMA
    shape = jax.ShapeDtypeStruct
    d_tok, d_gate, d_up, d_down = pl.pallas_call(
        layer,
        out_shape=(shape((TOK, width), BF16),) + (shape((hid, width), BF16),) * 3,
        in_specs=[anywhere, anywhere, vmem, anywhere, anywhere, anywhere],
        out_specs=(vmem, anywhere, anywhere, anywhere),
        scratch_shapes=[
            pltpu.VMEM((n, 2, NZ, PAD, w), BF16),
            pltpu.VMEM((n, 2, SRC, ROWS, w), BF16),
            pltpu.VMEM((n, 2, 2, ROWS, w), BF16),
            pltpu.VMEM((n, 2, 2, SRC, ROWS, w), BF16),
            pltpu.VMEM((2 * hid, width), BF16),
            pltpu.VMEM((hid, width), BF16),
            pltpu.VMEM((2 * hid, 4 * qr), F32),
            pltpu.VMEM((hid, 4 * qr), F32),
            pltpu.VMEM((2, 3, qr, qr), BF16),
            pltpu.VMEM((3, qr, qr), BF16),
            pltpu.VMEM((3, NZ, 16, 128), BF16),
            pltpu.VMEM((2, 3 * hid, 4 * qr), BF16),
            pltpu.VMEM((4 * qr, 2 * hid), BF16),
            pltpu.VMEM((half, 2, SRC, ROWS, w), BF16),
            pltpu.VMEM((half, 2, SRC, ROWS, w), BF16),
            pltpu.VMEM((half, 2, 2, ROWS, w), BF16),
            pltpu.VMEM((half, 7, 2, TOK, w), BF16),
            pltpu.VMEM((half, 2, TOK, w), BF16),
            pltpu.VMEM((half, TOK, w), BF16),
            pltpu.VMEM((2, 2 * hid, w), BF16),
            pltpu.VMEM((2, hid, w), BF16),
            dma((6,)), dma((n,)), dma((n,)), dma((n,)), dma((n, 7)), dma((n,)), dma((n,)), dma((n,)), dma((n,)),
            dma((n,)), dma((n,)), dma((9,)), dma((9,)),
            dma((half,)), dma((half,)), dma((half,)), dma((half,)), dma((half,)), dma((half,)), dma((half,)),
            dma((half, 7)), dma((half,)), dma((half,)), dma((2, 3)),
        ],
        compiler_params=pltpu.CompilerParams(collective_id=0, has_side_effects=True, vmem_limit_bytes=VMEM_LIMIT),
    )(tokens, out_grad, info, w_gate[0], w_up[0], w_down[0])
    return (d_tok, d_gate[None], d_up[None], d_down[None])


def solution(mesh):
    rows = P(("dp", "expert"), None)
    weights = P("expert", "dp", None)
    return jax.shard_map(
        per_device,
        mesh=mesh,
        in_specs=(rows, rows, rows, rows, weights, weights, weights),
        out_specs=(rows, weights, weights, weights),
        check_vma=False,
    )
```

```python
import jax
import jax.numpy as jnp
from jax import lax
from jax.experimental import pallas as pl
from jax.experimental.pallas import tpu as pltpu
from jax.sharding import PartitionSpec as P

MESH = pl.DeviceIdType.MESH
F32, BF16 = jnp.float32, jnp.bfloat16
VMEM_LIMIT = 67043328

NY, NX, NZ, NCORE = 4, 4, 8, 2
CAP = 4
TOK = 24
PAD = 32
SRC = NX * NCORE
ROWS = NZ * CAP
QUARTER = SRC * ROWS
WIDTH = 256
FAR, SELECT, LATE, MULTIPLY = 2, 4, 6, 11
SUM, TOKENS, RFAR, END, OUT = 4, 6, 8, 10, 16
DW_LAG = 2
REAL = pl.ds(0, TOK)


class Place:
    def __init__(self):
        self.y = lax.axis_index("dp")
        e = lax.axis_index("expert")
        self.c = lax.rem(e, NCORE)
        self.z = lax.rem(lax.div(e, NCORE), NZ)
        self.x = lax.div(e, NCORE * NZ)

    @staticmethod
    def first(i):
        return i + 1 - 2 * lax.rem(i, 2)

    @staticmethod
    def second(i):
        return 3 - i

    def pick(self, i, s):
        return (1 - s) * self.first(i) + s * self.second(i)

    def at(self, y=None, x=None, z=None, c=None):
        y = self.y if y is None else y
        x = self.x if x is None else x
        z = self.z if z is None else z
        c = self.c if c is None else c
        return (y, (x * NZ + z) * NCORE + c)

    def zz(self, d):
        return lax.rem(self.z + d + NZ, NZ)

    def enter(self):
        sem = pltpu.get_barrier_semaphore()
        peers = [self.at(y=self.first(self.y)), self.at(y=self.second(self.y)), self.at(c=1 - self.c)]
        peers += [self.at(z=self.zz(d)) for d in (1, -1, 2, -2)]
        for x in (self.first(self.x), self.second(self.x), lax.rem(self.x + 2, NX)):
            peers += [self.at(x=x, c=0), self.at(x=x, c=1)]
        for p in peers:
            pl.semaphore_signal(sem, inc=1, device_id=p, device_id_type=MESH)
        pl.semaphore_wait(sem, len(peers))


def send(src, dst, ssem, rsem, device):
    pltpu.make_async_remote_copy(
        src_ref=src, dst_ref=dst, send_sem=ssem, recv_sem=rsem, device_id=device, device_id_type=MESH
    ).start()


def await_(ref, sem):
    pltpu.make_async_copy(ref, ref, sem).wait()


def when(i, n):
    return pl.when(jnp.logical_and(i >= 0, i < n))


def dot(a, b, dims=((1,), (0,))):
    return lax.dot_general(a, b, (dims, ((), ())), preferred_element_type=F32)


def slot_exchange(p, sel, into, send_sem, recv_sem):
    mine = p.c
    for d, x in ((3, lax.rem(p.x + 2, NX)), (1, p.first(p.x)), (2, p.second(p.x))):
        for c in range(NCORE):
            send(sel.at[:, d * 2 + c], into.at[:, d * 2 + mine], send_sem, recv_sem, p.at(x=x, c=c))
    send(sel.at[:, 1 - mine], into.at[:, mine], send_sem, recv_sem, p.at(c=1 - mine))


def gather_near(p, block, ssem, rsem):
    mine = block(p.z)
    for j, d in enumerate((2, -2, 1, -1)):
        send(mine, mine, ssem(j), rsem.at[j], p.at(z=p.zz(d)))


def gather_far(p, s, block, ssem, rsem):
    for j in (0, 1):
        await_(block(p.z), rsem.at[j])
    d = 2 - 4 * s
    far = block(p.zz(-d))
    send(far, far, ssem(6), rsem.at[6], p.at(z=p.zz(d)))
    for j, d in enumerate((1, -1)):
        passed = block(p.zz(-2 * d))
        send(passed, passed, ssem(4 + j), rsem.at[4 + j], p.at(z=p.zz(d)))


def gather_wait(p, block, rsem):
    for j in range(2, 7):
        await_(block(p.z), rsem.at[j])


def quarter(pos, s):
    return (0, 1 + s, 2 - s, 3)[pos]


def select_matrices(p, rb, sm, st):
    lane = lax.broadcasted_iota(jnp.int32, (128, 128), 1)
    sub = lax.broadcasted_iota(jnp.int32, (128, 128), 0)
    before = jnp.where(jnp.logical_and(sub < lane, lax.div(sub, PAD) == lax.div(lane, PAD)), 1.0, 0.0).astype(BF16)
    r_row = lax.broadcasted_iota(jnp.int32, (ROWS, 128), 0)
    r_lane = lax.broadcasted_iota(jnp.int32, (ROWS, 128), 1)
    row_z, row_slot = lax.div(r_row, CAP), lax.rem(r_row, CAP).astype(F32)
    xs = (p.x, p.first(p.x), p.second(p.x), lax.rem(p.x + 2, NX))
    spread = lambda v: jnp.broadcast_to(v, (ROWS, 128))
    for role in range(3):
        for zh in range(2):
            both = rb[role, 4 * zh].astype(F32)
            for q in range(1, 4):
                both = both + rb[role, 4 * zh + q].astype(F32)
            route, gate = both[0:8].astype(jnp.int32), both[8:16]
            chosen, value = [], []
            for d in range(4):
                for c in range(NCORE):
                    hit = route == (xs[d] * NZ + p.z) * NCORE + c + 1
                    chosen.append(jnp.sum(jnp.where(hit, 1.0, 0.0), axis=0, keepdims=True))
                    value.append(jnp.sum(jnp.where(hit, gate, 0.0), axis=0, keepdims=True))
            chosen = jnp.concatenate(chosen, axis=0)
            earlier = dot(chosen.astype(BF16), before)
            same_z = row_z == 4 * zh + lax.div(r_lane, PAD)
            for e in range(SRC):
                hit = jnp.logical_and(spread(chosen[e : e + 1]) > 0.5, spread(earlier[e : e + 1]) == row_slot)
                hit = jnp.logical_and(same_z, hit)
                rows, cols = pl.ds(e * ROWS, ROWS), pl.ds(zh * 128, 128)
                sm[0, role, rows, cols] = jnp.where(hit, 1.0, 0.0).astype(BF16)
                sm[1, role, rows, cols] = jnp.where(hit, spread(value[e]), 0.0).astype(BF16)
        st[role] = sm[0, role].astype(F32).T.astype(BF16)


def layer(tok, ograd, info, wg, wu, wd, d_tok, d_w,
          zbuf, sel, rows, wgu, wdn, acc_gu, acc_d, sm, st, rb, act_t, act,
          got, back, zr, tail, tail_in, dw_gu, dw_d,
          sem_l, a_s, a_r, z_s, z_r, x_s, x_r, l_s, l_r, r_s, r_r,
          l2_s, l2_r, x2_s, x2_r, z2_s, z2_r, e_s, e_r, o_s):
    p = Place()
    n, w = zbuf.shape[0], zbuf.shape[-1]
    half = n // 2
    hid = wg.shape[0]
    qr = QUARTER

    def cols(i):
        return pl.ds(pl.multiple_of(i * w, w), w)

    own_info = pltpu.make_async_copy(info, rb.at[0, p.z], sem_l.at[0])
    own_info.start()
    for k, ref in enumerate((tok, ograd)):

        @pl.loop(0, half)
        def _(j, k=k, ref=ref):
            pltpu.make_async_copy(ref.at[:, cols(j)], zbuf.at[k * half + j, 0, p.z, REAL], sem_l.at[1 + k]).start()

    p.enter()
    send(info, rb.at[1, p.z], r_s.at[7], r_r.at[7], p.at(y=p.first(p.y)))
    send(info, rb.at[2, p.z], r_s.at[8], r_r.at[8], p.at(y=p.second(p.y)))
    for k, ref in enumerate((tok, ograd)):

        @pl.loop(0, half)
        def _(j, k=k, ref=ref):
            i = k * half + j
            to = p.at(y=p.pick(p.y, lax.rem(j, 2)))
            send(ref.at[:, cols(j)], zbuf.at[i, 1, p.z, REAL], a_s.at[i], a_r.at[i], to)

    loads = [
        pltpu.make_async_copy(wg, wgu.at[pl.ds(0, hid)], sem_l.at[3]),
        pltpu.make_async_copy(wu, wgu.at[pl.ds(hid, hid)], sem_l.at[4]),
        pltpu.make_async_copy(wd, wdn, sem_l.at[5]),
    ]
    for cp in loads:
        cp.start()

    zbuf[:, :, :, pl.ds(TOK, PAD - TOK), :] = jnp.zeros((n, 2, NZ, PAD - TOK, w), BF16)
    acc_gu[...] = jnp.zeros_like(acc_gu)
    acc_d[...] = jnp.zeros_like(acc_d)

    info_block = lambda z: rb.at[:, z]
    token_block = lambda i: lambda z: zbuf.at[i, :, z, REAL]

    def step(t, carry):
        i_far, i_sel, i_late, i_mul = t - FAR, t - SELECT, t - LATE, t - MULTIPLY

        @pl.when(t == 0)
        def _():
            own_info.wait()
            await_(info, r_r.at[7])
            await_(info, r_r.at[8])
            gather_near(p, info_block, lambda j: r_s.at[j], r_r)
            await_(tok, sem_l.at[1])

        @pl.when(t == FAR)
        def _():
            gather_far(p, 0, info_block, lambda j: r_s.at[j], r_r)

        @pl.when(t == SELECT)
        def _():
            gather_wait(p, info_block, r_r)
            select_matrices(p, rb, sm, st)

        @when(t, n)
        def _():
            @pl.when(t == half)
            def _():
                await_(ograd, sem_l.at[2])

            await_(tok.at[:, pl.ds(0, w)], a_r.at[t])
            gather_near(p, token_block(t), lambda j: z_s.at[t], z_r.at[t])

        @when(i_far, n)
        def _():
            gather_far(p, lax.rem(i_far, 2), token_block(i_far), lambda j: z_s.at[i_far], z_r.at[i_far])

        @when(i_sel, n)
        def _():
            s = lax.rem(i_sel, 2)
            which = lax.div(i_sel, half)
            gather_wait(p, token_block(i_sel), z_r.at[i_sel])
            for ys, role in ((0, 0), (1, 1 + s)):
                chosen = dot(sm[which, role], zbuf[i_sel, ys].reshape(NZ * PAD, w)).astype(BF16)
                sel[i_sel, ys] = chosen.reshape(SRC, ROWS, w)
            slot_exchange(p, sel.at[i_sel], rows.at[i_sel, 0], x_s.at[i_sel], x_r.at[i_sel])
            rows[i_sel, 0, :, p.c] = sel[i_sel, :, p.c]

        @when(i_late, n)
        def _():
            await_(rows.at[i_late, 0, :, pl.ds(0, 7)], x_r.at[i_late])
            late = p.at(y=p.pick(p.y, 1 - lax.rem(i_late, 2)))
            send(rows.at[i_late, 0], rows.at[i_late, 1], l_s.at[i_late], l_r.at[i_late], late)

        @pl.when(i_mul == 0)
        def _():
            for cp in loads:
                cp.wait()

        @when(i_mul, n)
        def _():
            s = lax.rem(i_mul, 2)
            await_(rows.at[i_mul, 1], l_r.at[i_mul])

            def multiply(acc, weights):
                part = weights[:, cols(lax.rem(i_mul, half))]
                for h in range(2):
                    for ys in range(2):
                        at = pl.ds(pl.multiple_of(quarter(2 * h + ys, s) * qr, qr), qr)
                        acc[:, at] += dot(part, rows[i_mul, h, ys].reshape(qr, w), ((1,), (1,)))

            @pl.when(i_mul < half)
            def _():
                multiply(acc_gu, wgu)

            @pl.when(i_mul >= half)
            def _():
                multiply(acc_d, wdn)

        return carry

    lax.fori_loop(0, n + MULTIPLY, step, 0)

    for q in range(4):
        at = pl.ds(q * qr, qr)
        swapped = pl.ds((0, 2, 1, 3)[q] * qr, qr)
        gate_pre, up_pre, d_hidden = acc_gu[0:hid, at], acc_gu[hid : 2 * hid, at], acc_d[:, at]
        sig = jax.nn.sigmoid(gate_pre)
        silu = gate_pre * sig
        d_up_act = d_hidden * silu
        d_gate_act = d_hidden * up_pre * sig * (1.0 + gate_pre * (1.0 - sig))
        both = jnp.concatenate([d_gate_act, d_up_act], axis=0)
        act[at, :] = both.T.astype(BF16)
        both, hidden = both.astype(BF16), (silu * up_pre).astype(BF16)
        for order, to in ((0, at), (1, swapped)):
            act_t[order, 0 : 2 * hid, to] = both
            act_t[order, 2 * hid : 3 * hid, to] = hidden

    @pl.loop(0, n)
    def _(i):
        await_(zbuf.at[i, :, pl.ds(0, 7), REAL], z_s.at[i])
        await_(sel.at[i, :, pl.ds(0, 7)], x_s.at[i])

    def part(i):
        return zbuf.at[i]

    def keep(i):
        return zbuf.at[half + i]

    def own(i):
        return sel.at[i]

    def sums(i):
        return sel.at[half + i]

    def back_step(t, carry):
        i_sum, i_tok, i_far, i_end, i_out = t - SUM, t - TOKENS, t - RFAR, t - END, t - OUT
        i_dw = t - DW_LAG

        @when(t, half)
        def _():
            s = lax.rem(t, 2)
            weights = wgu[:, cols(t)]
            for pos in (2, 3, 0, 1):
                a = act[pl.ds(pl.multiple_of(quarter(pos, s) * qr, qr), qr), :]
                value = dot(a, weights).astype(BF16).reshape(SRC, ROWS, w)
                if pos >= 2:
                    part(t)[pos - 2] = value
                else:
                    keep(t)[pos] = value
                if pos == 3:
                    send(part(t), got.at[t], l2_s.at[t], l2_r.at[t], p.at(y=p.pick(p.y, 1 - s)))

        @when(i_sum, half)
        def _():
            await_(got.at[i_sum], l2_r.at[i_sum])
            total = keep(i_sum)
            total[...] = (total[...].astype(F32) + got[i_sum].astype(F32)).astype(BF16)
            slot_exchange(p, total, back.at[i_sum], x2_s.at[i_sum], x2_r.at[i_sum])
            back[i_sum, :, p.c] = total[:, p.c]

        def z_send(i, j, src, d):
            send(src, zr.at[i, j], z2_s.at[i], z2_r.at[i, j], p.at(z=p.zz(d)))

        @when(i_tok, half)
        def _():
            s = lax.rem(i_tok, 2)
            await_(back.at[i_tok, :, pl.ds(0, 7)], x2_r.at[i_tok])
            mine = own(i_tok)
            for ys, role in ((0, 0), (1, 1 + s)):
                value = dot(st[role], back[i_tok, ys].reshape(qr, w)).astype(BF16)
                mine[ys] = value.reshape(NZ, PAD, w)
            d = 4 * s - 2
            z_send(i_tok, 2, mine.at[:, p.zz(4), REAL], d)
            for j, d in enumerate((-1, 1)):
                z_send(i_tok, j, mine.at[:, p.zz(3 * d), REAL], d)
                z_send(i_tok, 3 + j, mine.at[:, p.zz(d), REAL], d)

        @when(i_far, half)
        def _():
            s = lax.rem(i_far, 2)
            for j in range(3):
                await_(zr.at[i_far, j], z2_r.at[i_far, j])
            four = zr[i_far, 2].astype(F32)
            for j, d in enumerate((-2, 2)):
                value = own(i_far)[:, p.zz(d), REAL].astype(F32) + zr[i_far, j].astype(F32)
                value = value + jnp.where(s == j, four, 0.0)
                sums(i_far)[:, j, REAL] = value.astype(BF16)
                z_send(i_far, 5 + j, sums(i_far).at[:, j, REAL], d)

        @when(i_end, half)
        def _():
            for j in range(3, 7):
                await_(zr.at[i_end, j], z2_r.at[i_end, j])
            value = own(i_end)[:, p.z, REAL].astype(F32)
            for j in range(3, 7):
                value = value + zr[i_end, j].astype(F32)
            tail[i_end] = value.astype(BF16)
            send(tail.at[i_end, 1], tail_in.at[i_end], e_s.at[i_end], e_r.at[i_end], p.at(y=p.pick(p.y, lax.rem(i_end, 2))))

        @when(i_out, half)
        def _():
            await_(tail_in.at[i_out], e_r.at[i_out])
            value = tail[i_out, 0].astype(F32) + tail_in[i_out].astype(F32)
            d_tok[:, cols(i_out)] = value.astype(BF16)

        @when(i_dw, half)
        def _():
            slot = lax.rem(i_dw, 2)
            at = cols(i_dw)
            copies = (
                pltpu.make_async_copy(dw_gu.at[slot, pl.ds(0, hid)], d_w.at[pl.ds(0, hid), at], o_s.at[slot, 0]),
                pltpu.make_async_copy(dw_gu.at[slot, pl.ds(hid, hid)], d_w.at[pl.ds(hid, hid), at], o_s.at[slot, 1]),
                pltpu.make_async_copy(dw_d.at[slot], d_w.at[pl.ds(2 * hid, hid), at], o_s.at[slot, 2]),
            )

            @pl.when(i_dw >= 2)
            def _():
                for cp in copies:
                    cp.wait()

            a = act_t.at[slot]
            dw_gu[slot] = dot(a[0 : 2 * hid], rows[i_dw].reshape(4 * qr, w)).astype(BF16)
            dw_d[slot] = dot(a[2 * hid : 3 * hid], rows[half + i_dw].reshape(4 * qr, w)).astype(BF16)
            for cp in copies:
                cp.start()

        return carry

    lax.fori_loop(0, half + OUT, back_step, 0)

    @pl.loop(0, n)
    def _(i):
        await_(tok.at[:, pl.ds(0, w)], a_s.at[i])
        await_(rows.at[i, 0], l_s.at[i])

    @pl.loop(0, half)
    def _(i):
        await_(part(i), l2_s.at[i])
        await_(back.at[i, :, pl.ds(0, 7)], x2_s.at[i])
        await_(zr.at[i], z2_s.at[i])
        await_(tail_in.at[i], e_s.at[i])

    for slot in range(2):
        for j in range(3):
            await_(dw_d.at[slot], o_s.at[slot, j])
    for j in range(7):
        await_(rb.at[:, 0], r_s.at[j])
    await_(info, r_s.at[7])
    await_(info, r_s.at[8])


def per_device(tokens, out_grad, routes, gates, w_gate, w_up, w_down):
    width = tokens.shape[1]
    w = WIDTH
    half = width // w
    n = 2 * half
    hid = w_gate.shape[1]
    qr = QUARTER
    z = lax.rem(lax.div(lax.axis_index("expert"), NCORE), NZ)

    info = jnp.concatenate([(routes + 1).astype(BF16).T, gates.T], axis=0)
    info = jnp.pad(info, ((0, 0), (0, PAD - TOK)))
    info = jnp.where(lax.broadcasted_iota(jnp.int32, (16, 4, PAD), 1) == lax.rem(z, 4), info[:, None, :], 0).reshape(16, 128)

    anywhere = pl.BlockSpec(memory_space=pl.ANY)
    vmem = pl.BlockSpec(memory_space=pltpu.VMEM)
    dma = pltpu.SemaphoreType.DMA
    shape = jax.ShapeDtypeStruct
    d_tok, d_w = pl.pallas_call(
        layer,
        out_shape=(shape((TOK, width), BF16), shape((3 * hid, width), BF16)),
        in_specs=[anywhere, anywhere, vmem, anywhere, anywhere, anywhere],
        out_specs=(vmem, anywhere),
        scratch_shapes=[
            pltpu.VMEM((n, 2, NZ, PAD, w), BF16),
            pltpu.VMEM((n, 2, SRC, ROWS, w), BF16),
            pltpu.VMEM((n, 2, 2, SRC, ROWS, w), BF16),
            pltpu.VMEM((2 * hid, width), BF16),
            pltpu.VMEM((hid, width), BF16),
            pltpu.VMEM((2 * hid, 4 * qr), F32),
            pltpu.VMEM((hid, 4 * qr), F32),
            pltpu.VMEM((2, 3, qr, qr), BF16),
            pltpu.VMEM((3, qr, qr), BF16),
            pltpu.VMEM((3, NZ, 16, 128), BF16),
            pltpu.VMEM((2, 3 * hid, 4 * qr), BF16),
            pltpu.VMEM((4 * qr, 2 * hid), BF16),
            pltpu.VMEM((half, 2, SRC, ROWS, w), BF16),
            pltpu.VMEM((half, 2, SRC, ROWS, w), BF16),
            pltpu.VMEM((half, 7, 2, TOK, w), BF16),
            pltpu.VMEM((half, 2, TOK, w), BF16),
            pltpu.VMEM((half, TOK, w), BF16),
            pltpu.VMEM((2, 2 * hid, w), BF16),
            pltpu.VMEM((2, hid, w), BF16),
            dma((6,)), dma((n,)), dma((n,)), dma((n,)), dma((n, 7)), dma((n,)), dma((n,)), dma((n,)), dma((n,)),
            dma((9,)), dma((9,)),
            dma((half,)), dma((half,)), dma((half,)), dma((half,)), dma((half,)),
            dma((half, 7)), dma((half,)), dma((half,)), dma((2, 3)),
        ],
        compiler_params=pltpu.CompilerParams(collective_id=0, has_side_effects=True, vmem_limit_bytes=VMEM_LIMIT),
    )(tokens, out_grad, info, w_gate[0], w_up[0], w_down[0])
    return (d_tok, d_w[None, 0:hid], d_w[None, hid : 2 * hid], d_w[None, 2 * hid :])


def solution(mesh):
    rows = P(("dp", "expert"), None)
    weights = P("expert", "dp", None)
    return jax.shard_map(
        per_device,
        mesh=mesh,
        in_specs=(rows, rows, rows, rows, weights, weights, weights),
        out_specs=(rows, weights, weights, weights),
        check_vma=False,
    )
```

```python
import jax
import jax.numpy as jnp
from jax import lax
from jax.experimental import pallas as pl
from jax.experimental.pallas import tpu as pltpu
from jax.sharding import PartitionSpec as P

MESH = pl.DeviceIdType.MESH
F32, BF16 = jnp.float32, jnp.bfloat16
VMEM_LIMIT = 67043328

NY, NX, NZ, NCORE = 4, 4, 8, 2
CAP = 4
TOK = 24
PAD = 32
SRC = NX * NCORE
ROWS = NZ * CAP
QUARTER = SRC * ROWS
WIDTH = 256
FAR, SELECT, LATE, MULTIPLY = 2, 4, 6, 11
SUM, TOKENS, RFAR, END, OUT = 4, 6, 8, 10, 14
DW_LAG = 2
REAL = pl.ds(0, TOK)


class Place:
    def __init__(self):
        self.y = lax.axis_index("dp")
        e = lax.axis_index("expert")
        self.c = lax.rem(e, NCORE)
        self.z = lax.rem(lax.div(e, NCORE), NZ)
        self.x = lax.div(e, NCORE * NZ)

    @staticmethod
    def first(i):
        return i + 1 - 2 * lax.rem(i, 2)

    @staticmethod
    def second(i):
        return 3 - i

    def pick(self, i, s):
        return (1 - s) * self.first(i) + s * self.second(i)

    def at(self, y=None, x=None, z=None, c=None):
        y = self.y if y is None else y
        x = self.x if x is None else x
        z = self.z if z is None else z
        c = self.c if c is None else c
        return (y, (x * NZ + z) * NCORE + c)

    def zz(self, d):
        return lax.rem(self.z + d + NZ, NZ)

    def enter(self):
        sem = pltpu.get_barrier_semaphore()
        peers = [self.at(y=self.first(self.y)), self.at(y=self.second(self.y)), self.at(c=1 - self.c)]
        peers += [self.at(z=self.zz(d)) for d in (1, -1, 2, -2)]
        for x in (self.first(self.x), self.second(self.x), lax.rem(self.x + 2, NX)):
            peers += [self.at(x=x, c=0), self.at(x=x, c=1)]
        for p in peers:
            pl.semaphore_signal(sem, inc=1, device_id=p, device_id_type=MESH)
        pl.semaphore_wait(sem, len(peers))


def send(src, dst, ssem, rsem, device):
    pltpu.make_async_remote_copy(
        src_ref=src, dst_ref=dst, send_sem=ssem, recv_sem=rsem, device_id=device, device_id_type=MESH
    ).start()


def await_(ref, sem):
    pltpu.make_async_copy(ref, ref, sem).wait()


def when(i, n):
    return pl.when(jnp.logical_and(i >= 0, i < n))


def dot(a, b, dims=((1,), (0,))):
    return lax.dot_general(a, b, (dims, ((), ())), preferred_element_type=F32)


def slot_exchange(p, sel, into, send_sem, recv_sem):
    mine = p.c
    for d, x in ((3, lax.rem(p.x + 2, NX)), (1, p.first(p.x)), (2, p.second(p.x))):
        for c in range(NCORE):
            send(sel.at[:, d * 2 + c], into.at[:, d * 2 + mine], send_sem, recv_sem, p.at(x=x, c=c))
    send(sel.at[:, 1 - mine], into.at[:, mine], send_sem, recv_sem, p.at(c=1 - mine))


def gather_near(p, block, ssem, rsem):
    mine = block(p.z)
    for j, d in enumerate((2, -2, 1, -1)):
        send(mine, mine, ssem(j), rsem.at[j], p.at(z=p.zz(d)))


def gather_far(p, s, block, ssem, rsem):
    for j in (0, 1):
        await_(block(p.z), rsem.at[j])
    d = 2 - 4 * s
    far = block(p.zz(-d))
    send(far, far, ssem(6), rsem.at[6], p.at(z=p.zz(d)))
    for j, d in enumerate((1, -1)):
        passed = block(p.zz(-2 * d))
        send(passed, passed, ssem(4 + j), rsem.at[4 + j], p.at(z=p.zz(d)))


def gather_wait(p, block, rsem):
    for j in range(2, 7):
        await_(block(p.z), rsem.at[j])


def quarter(pos, s):
    return (0, 1 + s, 2 - s, 3)[pos]


def select_matrices(p, rb, sm, st):
    lane = lax.broadcasted_iota(jnp.int32, (128, 128), 1)
    sub = lax.broadcasted_iota(jnp.int32, (128, 128), 0)
    before = jnp.where(jnp.logical_and(sub < lane, lax.div(sub, PAD) == lax.div(lane, PAD)), 1.0, 0.0).astype(BF16)
    r_row = lax.broadcasted_iota(jnp.int32, (ROWS, 128), 0)
    r_lane = lax.broadcasted_iota(jnp.int32, (ROWS, 128), 1)
    row_z, row_slot = lax.div(r_row, CAP), lax.rem(r_row, CAP).astype(F32)
    xs = (p.x, p.first(p.x), p.second(p.x), lax.rem(p.x + 2, NX))
    spread = lambda v: jnp.broadcast_to(v, (ROWS, 128))
    for role in range(3):
        for zh in range(2):
            both = rb[role, 4 * zh].astype(F32)
            for q in range(1, 4):
                both = both + rb[role, 4 * zh + q].astype(F32)
            route, gate = both[0:8].astype(jnp.int32), both[8:16]
            chosen, value = [], []
            for d in range(4):
                for c in range(NCORE):
                    hit = route == (xs[d] * NZ + p.z) * NCORE + c + 1
                    chosen.append(jnp.sum(jnp.where(hit, 1.0, 0.0), axis=0, keepdims=True))
                    value.append(jnp.sum(jnp.where(hit, gate, 0.0), axis=0, keepdims=True))
            chosen = jnp.concatenate(chosen, axis=0)
            earlier = dot(chosen.astype(BF16), before)
            same_z = row_z == 4 * zh + lax.div(r_lane, PAD)
            for e in range(SRC):
                hit = jnp.logical_and(spread(chosen[e : e + 1]) > 0.5, spread(earlier[e : e + 1]) == row_slot)
                hit = jnp.logical_and(same_z, hit)
                rows, cols = pl.ds(e * ROWS, ROWS), pl.ds(zh * 128, 128)
                sm[0, role, rows, cols] = jnp.where(hit, 1.0, 0.0).astype(BF16)
                sm[1, role, rows, cols] = jnp.where(hit, spread(value[e]), 0.0).astype(BF16)
        st[role] = sm[0, role].astype(F32).T.astype(BF16)


def layer(tok, ograd, info, wg, wu, wd, d_tok, d_w,
          zbuf, sel, rows, wgu, wdn, acc_gu, acc_d, sm, st, rb, act_t, act,
          got, back, zr, tail, tail_in, dw_gu, dw_d,
          sem_l, a_s, a_r, z_s, z_r, x_s, x_r, l_s, l_r, r_s, r_r,
          l2_s, l2_r, x2_s, x2_r, z2_s, z2_r, e_s, e_r, o_s):
    p = Place()
    n, w = zbuf.shape[0], zbuf.shape[-1]
    half = n // 2
    hid = wg.shape[0]
    qr = QUARTER

    def cols(i):
        return pl.ds(pl.multiple_of(i * w, w), w)

    own_info = pltpu.make_async_copy(info, rb.at[0, p.z], sem_l.at[0])
    own_info.start()
    for k, ref in enumerate((tok, ograd)):

        @pl.loop(0, half)
        def _(j, k=k, ref=ref):
            pltpu.make_async_copy(ref.at[:, cols(j)], zbuf.at[k * half + j, 0, p.z, REAL], sem_l.at[1 + k]).start()

    p.enter()
    send(info, rb.at[1, p.z], r_s.at[7], r_r.at[7], p.at(y=p.first(p.y)))
    send(info, rb.at[2, p.z], r_s.at[8], r_r.at[8], p.at(y=p.second(p.y)))
    for k, ref in enumerate((tok, ograd)):

        @pl.loop(0, half)
        def _(j, k=k, ref=ref):
            i = k * half + j
            to = p.at(y=p.pick(p.y, lax.rem(j, 2)))
            send(ref.at[:, cols(j)], zbuf.at[i, 1, p.z, REAL], a_s.at[i], a_r.at[i], to)

    loads = [
        pltpu.make_async_copy(wg, wgu.at[pl.ds(0, hid)], sem_l.at[3]),
        pltpu.make_async_copy(wu, wgu.at[pl.ds(hid, hid)], sem_l.at[4]),
        pltpu.make_async_copy(wd, wdn, sem_l.at[5]),
    ]
    for cp in loads:
        cp.start()

    zbuf[:, :, :, pl.ds(TOK, PAD - TOK), :] = jnp.zeros((n, 2, NZ, PAD - TOK, w), BF16)
    acc_gu[...] = jnp.zeros_like(acc_gu)
    acc_d[...] = jnp.zeros_like(acc_d)

    info_block = lambda z: rb.at[:, z]
    token_block = lambda i: lambda z: zbuf.at[i, :, z, REAL]

    def step(t, carry):
        i_far, i_sel, i_late, i_mul = t - FAR, t - SELECT, t - LATE, t - MULTIPLY

        @when(i_late, n)
        def _():
            await_(rows.at[i_late, 0, :, pl.ds(0, 7)], x_r.at[i_late])
            late = p.at(y=p.pick(p.y, 1 - lax.rem(i_late, 2)))
            send(rows.at[i_late, 0], rows.at[i_late, 1], l_s.at[i_late], l_r.at[i_late], late)

        @pl.when(t == 0)
        def _():
            own_info.wait()
            await_(info, r_r.at[7])
            await_(info, r_r.at[8])
            gather_near(p, info_block, lambda j: r_s.at[j], r_r)
            await_(tok, sem_l.at[1])

        @pl.when(t == FAR)
        def _():
            gather_far(p, 0, info_block, lambda j: r_s.at[j], r_r)

        @pl.when(t == SELECT)
        def _():
            gather_wait(p, info_block, r_r)
            select_matrices(p, rb, sm, st)

        @when(i_sel, n)
        def _():
            s = lax.rem(i_sel, 2)
            which = lax.div(i_sel, half)
            gather_wait(p, token_block(i_sel), z_r.at[i_sel])
            for ys, role in ((0, 0), (1, 1 + s)):
                chosen = dot(sm[which, role], zbuf[i_sel, ys].reshape(NZ * PAD, w)).astype(BF16)
                sel[i_sel, ys] = chosen.reshape(SRC, ROWS, w)
            slot_exchange(p, sel.at[i_sel], rows.at[i_sel, 0], x_s.at[i_sel], x_r.at[i_sel])
            rows[i_sel, 0, :, p.c] = sel[i_sel, :, p.c]

        @when(i_far, n)
        def _():
            gather_far(p, lax.rem(i_far, 2), token_block(i_far), lambda j: z_s.at[i_far], z_r.at[i_far])

        @when(t, n)
        def _():
            @pl.when(t == half)
            def _():
                await_(ograd, sem_l.at[2])

            await_(tok.at[:, pl.ds(0, w)], a_r.at[t])
            gather_near(p, token_block(t), lambda j: z_s.at[t], z_r.at[t])

        @pl.when(i_mul == 0)
        def _():
            for cp in loads:
                cp.wait()

        @when(i_mul, n)
        def _():
            s = lax.rem(i_mul, 2)
            await_(rows.at[i_mul, 1], l_r.at[i_mul])
            await_(tok.at[:, pl.ds(0, w)], a_s.at[i_mul])
            await_(zbuf.at[i_mul, :, pl.ds(0, 7), REAL], z_s.at[i_mul])
            await_(sel.at[i_mul, :, pl.ds(0, 7)], x_s.at[i_mul])

            def multiply(acc, weights):
                part = weights[:, cols(lax.rem(i_mul, half))]
                for h in range(2):
                    for ys in range(2):
                        at = pl.ds(pl.multiple_of(quarter(2 * h + ys, s) * qr, qr), qr)
                        acc[:, at] += dot(part, rows[i_mul, h, ys].reshape(qr, w), ((1,), (1,)))

            @pl.when(i_mul < half)
            def _():
                multiply(acc_gu, wgu)

            @pl.when(i_mul >= half)
            def _():
                multiply(acc_d, wdn)

        return carry

    lax.fori_loop(0, n + MULTIPLY, step, 0)

    for q in range(4):
        at = pl.ds(q * qr, qr)
        swapped = pl.ds((0, 2, 1, 3)[q] * qr, qr)
        gate_pre, up_pre, d_hidden = acc_gu[0:hid, at], acc_gu[hid : 2 * hid, at], acc_d[:, at]
        sig = jax.nn.sigmoid(gate_pre)
        silu = gate_pre * sig
        d_up_act = d_hidden * silu
        d_gate_act = d_hidden * up_pre * sig * (1.0 + gate_pre * (1.0 - sig))
        both = jnp.concatenate([d_gate_act, d_up_act], axis=0)
        act[at, :] = both.T.astype(BF16)
        both, hidden = both.astype(BF16), (silu * up_pre).astype(BF16)
        for order, to in ((0, at), (1, swapped)):
            act_t[order, 0 : 2 * hid, to] = both
            act_t[order, 2 * hid : 3 * hid, to] = hidden

    def part(i):
        return zbuf.at[i]

    def keep(i):
        return zbuf.at[half + i]

    def own(i):
        return sel.at[i]

    def sums(i):
        return sel.at[half + i]

    def back_step(t, carry):
        i_sum, i_tok, i_far, i_end, i_out = t - SUM, t - TOKENS, t - RFAR, t - END, t - OUT
        i_dw = t - DW_LAG

        @when(t, half)
        def _():
            s = lax.rem(t, 2)
            weights = wgu[:, cols(t)]
            for pos in (2, 3, 0, 1):
                a = act[pl.ds(pl.multiple_of(quarter(pos, s) * qr, qr), qr), :]
                value = dot(a, weights).astype(BF16).reshape(SRC, ROWS, w)
                if pos >= 2:
                    part(t)[pos - 2] = value
                else:
                    keep(t)[pos] = value
                if pos == 3:
                    send(part(t), got.at[t], l2_s.at[t], l2_r.at[t], p.at(y=p.pick(p.y, 1 - s)))

        @when(i_sum, half)
        def _():
            await_(got.at[i_sum], l2_r.at[i_sum])
            total = keep(i_sum)
            total[...] = (total[...].astype(F32) + got[i_sum].astype(F32)).astype(BF16)
            slot_exchange(p, total, back.at[i_sum], x2_s.at[i_sum], x2_r.at[i_sum])
            back[i_sum, :, p.c] = total[:, p.c]

        def z_send(i, j, src, d):
            send(src, zr.at[i, j], z2_s.at[i], z2_r.at[i, j], p.at(z=p.zz(d)))

        @when(i_tok, half)
        def _():
            s = lax.rem(i_tok, 2)
            await_(back.at[i_tok, :, pl.ds(0, 7)], x2_r.at[i_tok])
            mine = own(i_tok)
            for ys, role in ((0, 0), (1, 1 + s)):
                value = dot(st[role], back[i_tok, ys].reshape(qr, w)).astype(BF16)
                mine[ys] = value.reshape(NZ, PAD, w)
            d = 4 * s - 2
            z_send(i_tok, 2, mine.at[:, p.zz(4), REAL], d)
            for j, d in enumerate((-1, 1)):
                z_send(i_tok, j, mine.at[:, p.zz(3 * d), REAL], d)
                z_send(i_tok, 3 + j, mine.at[:, p.zz(d), REAL], d)

        @when(i_far, half)
        def _():
            s = lax.rem(i_far, 2)
            for j in range(3):
                await_(zr.at[i_far, j], z2_r.at[i_far, j])
            await_(part(i_far), l2_s.at[i_far])
            four = zr[i_far, 2].astype(F32)
            for j, d in enumerate((-2, 2)):
                value = own(i_far)[:, p.zz(d), REAL].astype(F32) + zr[i_far, j].astype(F32)
                value = value + jnp.where(s == j, four, 0.0)
                sums(i_far)[:, j, REAL] = value.astype(BF16)
                z_send(i_far, 5 + j, sums(i_far).at[:, j, REAL], d)

        @when(i_end, half)
        def _():
            for j in range(3, 7):
                await_(zr.at[i_end, j], z2_r.at[i_end, j])
            await_(back.at[i_end, :, pl.ds(0, 7)], x2_s.at[i_end])
            value = own(i_end)[:, p.z, REAL].astype(F32)
            for j in range(3, 7):
                value = value + zr[i_end, j].astype(F32)
            tail[i_end] = value.astype(BF16)
            send(tail.at[i_end, 1], tail_in.at[i_end], e_s.at[i_end], e_r.at[i_end], p.at(y=p.pick(p.y, lax.rem(i_end, 2))))

        @when(i_out, half)
        def _():
            await_(tail_in.at[i_out], e_r.at[i_out])
            await_(zr.at[i_out], z2_s.at[i_out])
            await_(tail_in.at[i_out], e_s.at[i_out])
            value = tail[i_out, 0].astype(F32) + tail_in[i_out].astype(F32)
            d_tok[:, cols(i_out)] = value.astype(BF16)

        @when(i_dw, half)
        def _():
            slot = lax.rem(i_dw, 2)
            at = cols(i_dw)
            for k in (i_dw, half + i_dw):
                await_(rows.at[k, 0], l_s.at[k])
            copies = (
                pltpu.make_async_copy(dw_gu.at[slot, pl.ds(0, hid)], d_w.at[pl.ds(0, hid), at], o_s.at[slot, 0]),
                pltpu.make_async_copy(dw_gu.at[slot, pl.ds(hid, hid)], d_w.at[pl.ds(hid, hid), at], o_s.at[slot, 1]),
                pltpu.make_async_copy(dw_d.at[slot], d_w.at[pl.ds(2 * hid, hid), at], o_s.at[slot, 2]),
            )

            @pl.when(i_dw >= 2)
            def _():
                for cp in copies:
                    cp.wait()

            a = act_t.at[slot]
            dw_gu[slot] = dot(a[0 : 2 * hid], rows[i_dw].reshape(4 * qr, w)).astype(BF16)
            dw_d[slot] = dot(a[2 * hid : 3 * hid], rows[half + i_dw].reshape(4 * qr, w)).astype(BF16)
            for cp in copies:
                cp.start()

        return carry

    lax.fori_loop(0, half + OUT, back_step, 0)

    for slot in range(2):
        for j in range(3):
            await_(dw_d.at[slot], o_s.at[slot, j])
    for j in range(7):
        await_(rb.at[:, 0], r_s.at[j])
    await_(info, r_s.at[7])
    await_(info, r_s.at[8])


def per_device(tokens, out_grad, routes, gates, w_gate, w_up, w_down):
    width = tokens.shape[1]
    w = WIDTH
    half = width // w
    n = 2 * half
    hid = w_gate.shape[1]
    qr = QUARTER
    z = lax.rem(lax.div(lax.axis_index("expert"), NCORE), NZ)

    both = jnp.concatenate([(routes + 1).astype(BF16), gates], axis=1)
    token = lax.broadcasted_iota(jnp.int32, (TOK, 128), 0)
    lane = lax.broadcasted_iota(jnp.int32, (TOK, 128), 1)
    to_lane = (lane == token + PAD * lax.rem(z, 4)).astype(BF16)
    info = dot(both, to_lane, ((0,), (0,))).astype(BF16)

    anywhere = pl.BlockSpec(memory_space=pl.ANY)
    vmem = pl.BlockSpec(memory_space=pltpu.VMEM)
    dma = pltpu.SemaphoreType.DMA
    shape = jax.ShapeDtypeStruct
    d_tok, d_w = pl.pallas_call(
        layer,
        out_shape=(shape((TOK, width), BF16), shape((3 * hid, width), BF16)),
        in_specs=[anywhere, anywhere, vmem, anywhere, anywhere, anywhere],
        out_specs=(vmem, anywhere),
        scratch_shapes=[
            pltpu.VMEM((n, 2, NZ, PAD, w), BF16),
            pltpu.VMEM((n, 2, SRC, ROWS, w), BF16),
            pltpu.VMEM((n, 2, 2, SRC, ROWS, w), BF16),
            pltpu.VMEM((2 * hid, width), BF16),
            pltpu.VMEM((hid, width), BF16),
            pltpu.VMEM((2 * hid, 4 * qr), F32),
            pltpu.VMEM((hid, 4 * qr), F32),
            pltpu.VMEM((2, 3, qr, qr), BF16),
            pltpu.VMEM((3, qr, qr), BF16),
            pltpu.VMEM((3, NZ, 16, 128), BF16),
            pltpu.VMEM((2, 3 * hid, 4 * qr), BF16),
            pltpu.VMEM((4 * qr, 2 * hid), BF16),
            pltpu.VMEM((half, 2, SRC, ROWS, w), BF16),
            pltpu.VMEM((half, 2, SRC, ROWS, w), BF16),
            pltpu.VMEM((half, 7, 2, TOK, w), BF16),
            pltpu.VMEM((half, 2, TOK, w), BF16),
            pltpu.VMEM((half, TOK, w), BF16),
            pltpu.VMEM((2, 2 * hid, w), BF16),
            pltpu.VMEM((2, hid, w), BF16),
            dma((6,)), dma((n,)), dma((n,)), dma((n,)), dma((n, 7)), dma((n,)), dma((n,)), dma((n,)), dma((n,)),
            dma((9,)), dma((9,)),
            dma((half,)), dma((half,)), dma((half,)), dma((half,)), dma((half,)),
            dma((half, 7)), dma((half,)), dma((half,)), dma((2, 3)),
        ],
        compiler_params=pltpu.CompilerParams(collective_id=0, has_side_effects=True, vmem_limit_bytes=VMEM_LIMIT),
    )(tokens, out_grad, info, w_gate[0], w_up[0], w_down[0])
    return (d_tok, d_w[None, 0:hid], d_w[None, hid : 2 * hid], d_w[None, 2 * hid :])


def solution(mesh):
    rows = P(("dp", "expert"), None)
    weights = P("expert", "dp", None)
    return jax.shard_map(
        per_device,
        mesh=mesh,
        in_specs=(rows, rows, rows, rows, weights, weights, weights),
        out_specs=(rows, weights, weights, weights),
        check_vma=False,
    )
```
